512 devices in a mesh: space: 64 (over y, z), mode: 8 (over x, core).
Axes of the slice: x: 4, y: 4, z: 16, core: 2. Of those that a mesh axis runs over, the one named last changes fastest.
Arguments:
- guess: float32 [120, 128, 8, 128], P('mode', 'space'), may hold values from -6 to 6
- source: float32 [120, 128, 8, 128], P('mode', 'space'), may hold values from -6 to 6
- mean_coef: float32 [128, 8, 128], P('space'), may hold values from 1 to 4
- fluct_coef: float32 [7, 128, 8, 128], P(None, 'space'), may hold values from -2 to 2
- triples: int32 [3, 1680], replicated, may hold values from 0 to 119, as said below
- coupling: float32 [1680], replicated, may hold values from -1.5 to 1.5
Outputs:
- solution: float32 [120, 128, 8, 128], P('mode', 'space')
- update: float32 [120, 128, 8, 128], P('mode', 'space')
The draws below stay inside these ranges and needn't reach their ends.
Inputs may be any that keep to these rules, and one draw needn't show every extreme that they name: `triples`: row 0 holds the output mode i, row 1 the coupled mode j, row 2 the term k, which is 1 to 7; every pair (i, k) stands in exactly 2 entries, in no particular order; j is any mode.
All inputs are finite; a program needn't handle non-finite values.
Results may differ from the reference program's by a relative error of at most 0.00019.
Values sent between devices are 32-bit elements; how exact they have to be, the bound alone decides.
No kernel may reach another device: no remote copies, remote signals or barrier semaphores. Data moves between devices by JAX's collectives and lax.ppermute only.
A program may use at most 64 MiB of HBM per device.

```python
import math
import jax
import jax.numpy as jnp
from jax import lax

P_SIZE = 120
KT = 8
S = 2
CY = 8
CZ = 128
ITERS = 3
NX = 128
NNZ = 1680


def draw_triples(key, part):
    count = P_SIZE * (KT - 1) * S
    order = jax.random.permutation(jax.random.fold_in(key, 11), count)
    first = order // ((KT - 1) * S)
    term = 1 + order // S % (KT - 1)
    partner = jax.random.randint(jax.random.fold_in(key, 12), (count,), 0, P_SIZE)
    return jnp.stack([first, partner, term]).astype(jnp.int32)


def block_scale(rng, dims, cuts, least, high):
    loudness = 1.0
    for dim, blocks in cuts:
        draws = jax.random.uniform(jax.random.fold_in(jax.random.fold_in(rng, 6), dim), (blocks,), jnp.float32, least / len(cuts), high / len(cuts))
        loudness = loudness * jnp.repeat(jnp.exp(draws), dims[dim] // blocks).reshape((-1,) + (1,) * (len(dims) - 1 - dim))
    return loudness


def scatter_about(own_key, shape, spread, reach, cuts=(), kind=jnp.bfloat16):
    array = spread * jax.random.normal(own_key, shape, jnp.float32)
    if cuts:
        array = array * block_scale(own_key, shape, cuts, -0.22, 0.18)
    return jnp.clip(array, -reach, reach).astype(kind)


def setup_inputs(seed: int = 0) -> dict:
    keys = jax.random.split(jax.random.key(seed), 7)
    return {
        "guess": scatter_about(keys[0], (P_SIZE, NX, CY, CZ), 1.0, 6.0, ((0, 8), (1, 64)), jnp.float32),
        "source": scatter_about(keys[1], (P_SIZE, NX, CY, CZ), 1.0, 6.0, ((0, 8), (1, 64)), jnp.float32),
        "mean_coef": jnp.clip(jnp.exp(math.log(4.0) - 1.3862944 * jax.random.uniform(keys[2], (NX, CY, CZ), jnp.float32) ** block_scale(keys[2], (NX, CY, CZ), ((0, 64),), -0.2, 0.2)), 1.0, 4.0),
        "fluct_coef": scatter_about(keys[3], (KT - 1, NX, CY, CZ), 0.4, 2.0, ((1, 64),), jnp.float32),
        "triples": draw_triples(jax.random.fold_in(keys[6], 71), 0),
        "coupling": scatter_about(keys[5], (NNZ,), 0.3, 1.5, (), jnp.float32),
    }


def neighbours(padded):
    centre = padded[..., 1:-1, 1:-1, 1:-1]
    others = [padded[..., 2:, 1:-1, 1:-1], padded[..., :-2, 1:-1, 1:-1],
              padded[..., 1:-1, 2:, 1:-1], padded[..., 1:-1, :-2, 1:-1],
              padded[..., 1:-1, 1:-1, 2:], padded[..., 1:-1, 1:-1, :-2]]
    return centre, others


def face_terms(padded_coef):
    centre, others = neighbours(padded_coef)
    return [0.5 * (centre + other) for other in others]


def reference(guess, source, mean_coef, fluct_coef, triples, coupling):
    coefs = jnp.concatenate([mean_coef[None], fluct_coef], axis=0)
    faces = face_terms(jnp.pad(coefs, ((0, 0), (1, 1), (1, 1), (1, 1))))
    diagonal = faces[0][0]
    for face in faces[1:]:
        diagonal = diagonal + face[0]
    table = jnp.zeros((P_SIZE, KT, P_SIZE), jnp.float32).at[triples[0], triples[2], triples[1]].add(coupling)
    table = table.at[:, 0, :].add(jnp.eye(P_SIZE, dtype=jnp.float32))
    solution = guess
    update = guess
    for step in range(ITERS):
        flat = solution.reshape(P_SIZE, -1)

        def one_mode(row):
            mixed = jnp.dot(row, flat, precision=lax.Precision.HIGHEST).reshape((KT,) + solution.shape[1:])
            padded = jnp.pad(mixed, ((0, 0), (1, 1), (1, 1), (1, 1)))
            centre, others = neighbours(padded)
            total = jnp.zeros(solution.shape[1:], jnp.float32)
            for face, other in zip(faces, others):
                total = total + jnp.sum(face * (centre - other), axis=0)
            return total

        image = lax.map(one_mode, table)
        update = (source - image) / diagonal
        solution = solution + 0.5 * update
    return (solution, update)
```

```python
import jax
import jax.numpy as jnp
import numpy as np
from jax import lax
from jax.experimental import pallas as pl
from jax.experimental.pallas import tpu as pltpu
from jax.sharding import PartitionSpec as P

ITERS = 3
PARTS = 8
BLOCK = 15
MODES = 120
TERMS = 8
Y, Z = 8, 128
ZW = 16
TRI = 5
ROWS = 11

GW, FW, MW = 22, 20, 84


def _segments():
    first, second = [], []
    for plane, low, width in ((0, -2, 20), (1, -2, 20), (-1, -1, 18), (2, -1, 18), (-2, 0, 16), (3, 0, 16)):
        first += [(plane, low + t) for t in range(width)]
    for plane, low, high in ((0, -3, 18), (1, -3, 18), (-1, -2, 17), (2, -2, 17), (-2, -1, 16), (3, -1, 16)):
        second += [(plane, low), (plane, high)]
    for plane in (-3, 4):
        second += [(plane, t) for t in range(ZW)]
    return first, second


def _tables():
    first, second = _segments()
    at0 = {cell: lane for lane, cell in enumerate(first)}
    at1 = {cell: lane for lane, cell in enumerate(second)}

    def g_lane(r, plane, z):
        return (MW * r + GW * plane + z + 3) % 128

    def f_lane(r, plane, z):
        return (MW * r + 2 * GW + FW * plane + z + 2) % 128

    def origin(plane):
        if plane in (0, 1):
            return 0, plane
        if plane in (-2, -1):
            return 1, plane + 2
        return 2, plane - 2

    rows = []

    def add(fill):
        row = np.zeros(128, np.int32)
        for lane, value in fill:
            row[lane] = value
        rows.append(row)
        return len(rows) - 1

    name = {}
    name["v0"] = [add([(l, g_lane(r, origin(p)[1], z)) for l, (p, z) in enumerate(first)]) for r in range(3)]
    name["f"] = [add([(l, f_lane(r, origin(p)[1], z)) for l, (p, z) in enumerate(first)]) for r in range(3)]
    inner = [(l, c) for l, c in enumerate(second) if c[0] not in (-3, 4)]
    name["v1"] = [add([(l, g_lane(r, origin(p)[1], z)) for l, (p, z) in inner]) for r in range(3)]
    name["code0"] = add([(l, origin(p)[0]) for l, (p, z) in enumerate(first)])
    name["code1"] = add([(l, {-3: 3, 4: 4}.get(p, origin(p)[0])) for l, (p, z) in enumerate(second)])
    name["near0"], name["near1"], name["which"] = [], [], []
    for dp, dz in ((0, 1), (0, -1), (1, 0), (-1, 0)):
        zero, one, mask = [], [], []
        for l, (p, z) in enumerate(first):
            cell = (p + dp, z + dz)
            if cell in at0:
                zero.append((l, at0[cell]))
            else:
                one.append((l, at1[cell]))
                mask.append((l, 1))
        name["near0"].append(add(zero))
        name["near1"].append(add(one))
        name["which"].append(add(mask))
    own = []
    for l in range(128):
        q = l % 32
        own.append((l, at0[(q // 16, q % 16)]))
    name["own"] = add(own)
    while len(rows) % 8:
        rows.append(np.zeros(128, np.int32))
    return np.stack(rows), name


TABLE, AT = _tables()


def _take(tile, index):
    return jnp.take_along_axis(tile, index, axis=1, mode="promise_in_bounds")


def _lane():
    return lax.broadcasted_iota(jnp.int32, (Y, 128), 1)


def _roll(tile, amount):
    amount %= 128
    return pltpu.roll(tile, amount, 1) if amount else tile


def _send_kernel(which_ref, guess_ref, source_ref, mean_ref, fluct_ref, out_ref):
    lane = _lane()

    def trimmed(tile, d, offset):
        if d == 0:
            tile = jnp.where(offset < 0, 0.0, tile)
        if d == PARTS - 1:
            tile = jnp.where(offset >= ZW, 0.0, tile)
        return tile

    def offsets(lanes):
        q = lanes % MW
        g = q % GW - 3
        f = (q - 2 * GW) % FW - 2
        return jnp.where(q < 2 * GW, g, f)

    low, high = offsets(lane), offsets(lane + 128)

    def triple(t, _):
        m = 3 * t
        a, b, c = ([(guess_ref[m + r, p], source_ref[m + r, p]) for p in range(2)] for r in range(3))
        for d in range(PARTS):
            base = -ZW * d
            parts = [
                (0, a[0][0], 3), (22, a[1][0], 25), (44, a[0][1], 46), (64, a[1][1], 66),
                (84, b[0][0], 87), (106, b[1][0], 109),
            ]
            tile = _roll(parts[0][1], parts[0][2] + base)
            for start, piece, shift in parts[1:]:
                tile = jnp.where(lane >= start, _roll(piece, shift + base), tile)
            out_ref[d, 2 * t] = trimmed(tile, d, low)
            parts = [
                (0, b[0][1], 2), (20, b[1][1], 22), (40, c[0][0], 43), (62, c[1][0], 65),
                (84, c[0][1], 86), (104, c[1][1], 106),
            ]
            tile = _roll(parts[0][1], parts[0][2] + base)
            for start, piece, shift in parts[1:]:
                tile = jnp.where(lane >= start, _roll(piece, shift + base), tile)
            out_ref[d, 2 * t + 1] = trimmed(tile, d, high)
        return 0

    lax.fori_loop(0, TRI, triple, 0)
    which = which_ref[0]
    other = jnp.maximum(which - 1, 0)
    coef = [jnp.where(which == 0, mean_ref[p], fluct_ref[other, p]) for p in range(2)]
    offset = lane % GW - 3
    for d in range(PARTS):
        tile = jnp.where(lane >= GW, _roll(coef[1], 25 - ZW * d), _roll(coef[0], 3 - ZW * d))
        out_ref[d, ROWS - 1] = trimmed(tile, d, offset)


def _far_kernel(block_ref, right_ref, left_ref):
    lane = _lane()

    def per_block(s, _):
        for plane, out_ref in ((1, right_ref), (0, left_ref)):
            for half in range(2):
                tile = None
                for q in range(8):
                    m = 8 * half + q
                    t, r = divmod(m, 3)
                    row = ROWS - 1 if m == 15 else 2 * t + (r == 2)
                    start = 3 + GW * plane + (0 if m == 15 else (MW * r) % 128)
                    piece = _roll(block_ref[s, row], 16 * q - start)
                    tile = piece if tile is None else jnp.where(lane >= 16 * q, piece, tile)
                out_ref[s, half] = tile
        return 0

    lax.fori_loop(0, PARTS, per_block, 0)


def _sweep_kernel(
    j1_ref, j2_ref, c1_ref, c2_ref, table_ref, own_ref, left_ref, right_ref, left2_ref, right2_ref,
    out_ref, s0_ref, s1_ref, t0_ref, ls_ref, f_ref, a0_ref, a1_ref, b_ref,
):
    lane = _lane()

    def row(at):
        return jnp.broadcast_to(table_ref[pl.ds(at, 1), :], (Y, 128))

    y = lax.broadcasted_iota(jnp.int32, (Y, 128), 0)
    inner_up = (y > 0).astype(jnp.float32)
    inner_down = (y < Y - 1).astype(jnp.float32)

    def along_y(x):
        return pltpu.roll(x, 1, 0) * inner_up + pltpu.roll(x, Y - 1, 0) * inner_down

    def near(x0, x1=None):
        total = along_y(x0)
        for n in range(4):
            piece = _take(x0, row(AT["near0"][n]))
            if x1 is not None:
                piece = jnp.where(row(AT["which"][n]) != 0, _take(x1, row(AT["near1"][n])), piece)
            total = total + piece
        return total

    def gathered(s, rows, index, code):
        tile = _take(own_ref[s, rows], index)
        tile = jnp.where(code == 1, _take(left_ref[s, rows], index), tile)
        return jnp.where(code == 2, _take(right_ref[s, rows], index), tile)

    def pair(s, rows, r, half, q):
        code0, code1 = row(AT["code0"]), row(AT["code1"])
        first = gathered(s, rows, row(AT["v0"][r]), code0)
        second = gathered(s, rows, row(AT["v1"][r]), code1)
        second = jnp.where(code1 == 3, _roll(left2_ref[s, half], 12 - 16 * q), second)
        second = jnp.where(code1 == 4, _roll(right2_ref[s, half], 28 - 16 * q), second)
        return first, jnp.where(lane < 44, second, 0.0)

    def unpack(s, _):
        for m in range(BLOCK):
            t, r = divmod(m, 3)
            first, second = pair(s, 2 * t + (r == 2), r, m // 8, m % 8)
            s0_ref[s * BLOCK + m] = first
            s1_ref[s * BLOCK + m] = second
            f_ref[s * BLOCK + m] = 2.0 * gathered(s, 2 * t + (r > 0), row(AT["f"][r]), row(AT["code0"]))
        first, second = pair(s, ROWS - 1, 0, 1, 7)
        a0_ref[s] = first
        a1_ref[s] = second
        b_ref[s] = 6.0 * first + near(first, second)
        return 0

    lax.fori_loop(0, PARTS, unpack, 0)
    mean = a0_ref[0]
    inside = mean > 0.0
    b_ref[TERMS] = jnp.where(inside, 1.0 / jnp.where(inside, b_ref[0], 1.0), 0.0)

    def neighbours_of(src_ref, wide):
        def body(j, _):
            ls_ref[j] = near(src_ref[j], s1_ref[j] if wide else None)
            return 0

        lax.fori_loop(0, MODES, body, 0, unroll=4)

    def sweep(src_ref, dst_ref, wide, last):
        neighbours_of(src_ref, wide)

        def body(i, _):
            mine = src_ref[i]
            u0 = a0_ref[0] * mine
            u1 = a1_ref[0] * s1_ref[i] if wide else None
            v = b_ref[0] * mine - a0_ref[0] * ls_ref[i]
            for k in range(1, TERMS):
                at = i * (TERMS - 1) + (k - 1)
                j1, j2, c1, c2 = j1_ref[at], j2_ref[at], c1_ref[at], c2_ref[at]
                m0 = c1 * src_ref[j1] + c2 * src_ref[j2]
                lm = c1 * ls_ref[j1] + c2 * ls_ref[j2]
                a0 = a0_ref[k]
                u0 = u0 + a0 * m0
                v = v + (b_ref[k] * m0 - a0 * lm)
                if wide:
                    u1 = u1 + a1_ref[k] * (c1 * s1_ref[j1] + c2 * s1_ref[j2])
            update = (f_ref[i] - v + near(u0, u1)) * b_ref[TERMS]
            dst_ref[i] = mine + 0.5 * update
            if last:
                f_ref[i] = update
            return 0

        lax.fori_loop(0, MODES, body, 0, unroll=2)

    sweep(s0_ref, t0_ref, True, False)
    sweep(t0_ref, s0_ref, False, False)
    sweep(s0_ref, t0_ref, False, True)

    def pack(d, _):
        index = row(AT["own"])
        for q in range(8):
            m = d * BLOCK + 2 * q
            tile = jnp.where(lane < 32, _take(t0_ref[m], index), _take(f_ref[m], index))
            if q < 7:
                tile = jnp.where(lane >= 64, _take(t0_ref[m + 1], index), tile)
                tile = jnp.where(lane >= 96, _take(f_ref[m + 1], index), tile)
            out_ref[d, q] = tile
        return 0

    lax.fori_loop(0, PARTS, pack, 0)


def _receive_kernel(piece_ref, solution_ref, update_ref):
    lane = _lane()

    def per_pair(q, _):
        tiles = [piece_ref[d, q] for d in range(PARTS)]
        for r in range(2):
            for n in range(4):
                tile = _roll(tiles[0], -64 * r - 16 * n)
                for d in range(1, PARTS):
                    tile = jnp.where(lane >= 16 * d, _roll(tiles[d], 16 * d - 64 * r - 16 * n), tile)
                out_ref = (solution_ref, update_ref)[n // 2]

                @pl.when(2 * q + r < BLOCK)
                def _():
                    out_ref[jnp.minimum(2 * q + r, BLOCK - 1), n % 2] = tile

        return 0

    lax.fori_loop(0, 8, per_pair, 0)


def _vmem(count):
    return [pl.BlockSpec(memory_space=pltpu.VMEM)] * count


def _smem(count):
    return [pl.BlockSpec(memory_space=pltpu.SMEM)] * count


def pattern_tables(triples, coupling):
    entries = coupling.shape[0]
    key = triples[0] * (TERMS - 1) + triples[2] - 1
    slots = lax.iota(jnp.int32, MODES * (TERMS - 1))
    code = lax.iota(jnp.int32, entries) * 128 + triples[1]
    match = key[:, None] == slots[None, :]
    low = jnp.min(jnp.where(match, code[:, None], entries * 128), axis=0)
    high = jnp.max(jnp.where(match, code[:, None], -1), axis=0)
    c1 = jnp.sum(jnp.where(code[:, None] == low[None, :], coupling[:, None], 0.0), axis=0)
    c2 = jnp.sum(jnp.where(code[:, None] == high[None, :], coupling[:, None], 0.0), axis=0)
    return low % 128, high % 128, c1, c2


def per_device(guess, source, mean_coef, fluct_coef, triples, coupling):
    f32 = jnp.float32
    which = lax.axis_index("mode").astype(jnp.int32).reshape(1)
    message = pl.pallas_call(
        _send_kernel,
        out_shape=jax.ShapeDtypeStruct((PARTS, ROWS, Y, 128), f32),
        in_specs=_smem(1) + _vmem(4),
        out_specs=_vmem(1)[0],
        name="send",
    )(which, guess, source, mean_coef, fluct_coef)
    block = lax.all_to_all(message, "mode", 0, 0, tiled=True)
    far_right, far_left = pl.pallas_call(
        _far_kernel,
        out_shape=[jax.ShapeDtypeStruct((PARTS, 2, Y, 128), f32)] * 2,
        in_specs=_vmem(1),
        out_specs=_vmem(2),
        name="far",
    )(block)
    count = lax.axis_size("space")

    def up(x, by):
        return lax.ppermute(x, "space", [(n, n + by) for n in range(count - by)])

    def down(x, by):
        return lax.ppermute(x, "space", [(n + by, n) for n in range(count - by)])

    from_left, from_right = up(block, 1), down(block, 1)
    from_left2, from_right2 = up(far_right, 2), down(far_left, 2)
    j1, j2, c1, c2 = pattern_tables(triples, coupling)
    tile = (Y, 128)
    result = pl.pallas_call(
        _sweep_kernel,
        out_shape=jax.ShapeDtypeStruct((PARTS, 8, Y, 128), f32),
        in_specs=_smem(4) + _vmem(6),
        out_specs=_vmem(1)[0],
        scratch_shapes=[pltpu.VMEM((MODES,) + tile, f32)] * 5
        + [pltpu.VMEM((TERMS,) + tile, f32)] * 2
        + [pltpu.VMEM((TERMS + 1,) + tile, f32)],
        name="sweeps",
    )(j1, j2, c1, c2, jnp.asarray(TABLE), block, from_left, from_right, from_left2, from_right2)
    pieces = lax.all_to_all(result, "mode", 0, 0, tiled=True)
    return tuple(
        pl.pallas_call(
            _receive_kernel,
            out_shape=[jax.ShapeDtypeStruct(guess.shape, f32)] * 2,
            in_specs=_vmem(1),
            out_specs=_vmem(2),
            name="receive",
        )(pieces)
    )


def solution(mesh):
    in_specs = (
        P("mode", "space", None, None),
        P("mode", "space", None, None),
        P("space", None, None),
        P(None, "space", None, None),
        P(),
        P(),
    )
    out_specs = (P("mode", "space", None, None), P("mode", "space", None, None))
    return jax.shard_map(
        per_device, mesh=mesh, in_specs=in_specs, out_specs=out_specs, check_vma=False
    )
```

```python
import jax
import jax.numpy as jnp
import numpy as np
from jax import lax
from jax.experimental import pallas as pl
from jax.experimental.pallas import tpu as pltpu
from jax.sharding import Mesh
from jax.sharding import PartitionSpec as P

ITERS = 3
SLABS = 2
PARTS = 8
GROUP = SLABS * PARTS
BLOCK = 15
MODES = 120
TERMS = 8
Y, Z = 8, 128
ZW = 8
PW = 14
SLOT = 64
F32 = jnp.float32


def _lane_of(plane, z):
    if plane == -3:
        return 112 + z
    if plane == 6:
        return 120 + z
    return PW * (plane + 2) + z + 3


def _near_matrix():
    cells = {}
    for plane in range(-2, 6):
        for z in range(-3, 11):
            cells[plane, z] = _lane_of(plane, z)
    for plane in (-3, 6):
        for z in range(ZW):
            cells[plane, z] = _lane_of(plane, z)
    near = np.zeros((128, 128), np.float32)
    for (plane, z), lane in cells.items():
        for cell in ((plane + 1, z), (plane - 1, z), (plane, z + 1), (plane, z - 1)):
            if cell in cells:
                near[cells[cell], lane] = 1.0
    return np.concatenate([near] * 3, axis=0)


G_PARTS = ((-2, 12), (-1, 10), (0, 8))
F_PARTS = ((-1, 10), (0, 8))
G_FROM = {"right": (PW + 1, 2, 56), "left": (1, PW + 2, 56)}
F_FROM = {"right": (3 * PW + 2, 2 * PW + 3), "left": (2 * PW + 2, 3 * PW + 3)}


def _tables():
    rows, at = [], {}

    def add(name, fill):
        row = np.zeros(128, np.int32)
        for lane, value in fill:
            row[lane] = value
        at[name] = len(rows)
        rows.append(row)

    def f_place(j):
        if j < 6:
            return (2, 18 * j), (2, 18 * j + 10)
        return (2, 108 + 10 * (j - 6)), (j - 6, 120)

    for way in ("right", "left"):
        index = [[], [], []]
        source = [[], [], []]
        for j in range(8):
            base, row = SLOT * (j % 2), j // 2
            lane = 30 * (j % 4)
            for start, (_, width) in zip(G_FROM[way], G_PARTS):
                for t in range(width):
                    index[j // 4].append((lane, base + start + t))
                    source[j // 4].append((lane, row))
                    lane += 1
            for start, (_, width), (tile, lane) in zip(F_FROM[way], F_PARTS, f_place(j)):
                for t in range(width):
                    index[tile].append((lane + t, base + start + t))
                    source[tile].append((lane + t, row))
        for w in range(3):
            add(("pack", way, w), index[w])
            add(("from", w), source[w])
    sides = ((-1, -2, -3), (4, 5, 6))
    for pos in range(4):
        fill = []
        for planes in sides:
            lane = 30 * pos
            for plane, (low, width) in zip(planes, G_PARTS):
                for t in range(width):
                    fill.append((_lane_of(plane, low + t), lane))
                    lane += 1
        add(("g", pos), fill)
    for j in range(8):
        fill = []
        for planes in sides:
            for plane, (low, width), (_, lane) in zip(planes, F_PARTS, f_place(j)):
                fill += [(_lane_of(plane, low + t), lane + t) for t in range(width)]
        add(("f", j), fill)
    for slab in range(SLABS):
        fill = []
        for lane in range(128):
            part, z = lane % 32 // ZW, lane % ZW
            home = _lane_of(SLABS * slab + part % 2, z)
            fill.append((lane, (home + SLOT * (part // 2)) % 128))
        add(("own", slab), fill)
    while len(rows) % 8:
        rows.append(np.zeros(128, np.int32))
    return np.stack(rows), at


TABLE, AT = _tables()
NEAR = _near_matrix()


def _take(tile, index):
    return jnp.take_along_axis(tile, index, axis=1, mode="promise_in_bounds")


def _lane():
    return lax.broadcasted_iota(jnp.int32, (Y, 128), 1)


def _roll(tile, amount):
    amount %= 128
    return pltpu.roll(tile, amount, 1) if amount else tile


def _send_kernel(which_ref, guess_ref, source_ref, mean_ref, fluct_ref, out_ref):
    lane = _lane()
    off = lane % SLOT % PW - 3
    which = which_ref[0]
    other = jnp.maximum(which - 1, 0)
    for t in range(PARTS):
        pieces = []
        for r in range(2):
            m = 2 * t + r
            if m < BLOCK:
                four = (guess_ref[m, 0], guess_ref[m, 1], source_ref[m, 0], source_ref[m, 1])
            else:
                four = tuple(jnp.where(which == 0, mean_ref[p], fluct_ref[other, p]) for p in range(2))
            for n, piece in enumerate(four):
                start = SLOT * r + PW * n
                pieces.append((start, _roll(piece, start + 3)))
        for q in range(GROUP):
            shifted = (lane - ZW * q) & 127
            tile = pieces[0][1]
            for start, piece in pieces[1:]:
                tile = jnp.where(shifted >= start, piece, tile)
            tile = _roll(tile, -ZW * q)
            if q == 0:
                tile = jnp.where(off < 0, 0.0, tile)
            if q == GROUP - 1:
                tile = jnp.where(off >= ZW, 0.0, tile)
            out_ref[q, t] = tile


def _halo_kernel(table_ref, block_ref, right_ref, left_ref):
    spare = _lane() % SLOT >= 4 * PW

    def row(name):
        return jnp.broadcast_to(table_ref[pl.ds(AT[name], 1), :], (Y, 128))

    for way, out_ref in (("right", right_ref), ("left", left_ref)):
        home, away, shift = (PARTS, 0, 56 - 17) if way == "right" else (0, PARTS, 56 - 3)
        for half in range(2 * PARTS):
            md, h = divmod(half, 2)
            merged = []
            for t in range(4 * h, 4 * h + 4):
                merged.append(jnp.where(spare, _roll(block_ref[away + md, t], shift), block_ref[home + md, t]))
            for w, sources in ((0, (0, 1, 3)), (1, (2, 3)), (2, (0, 1, 2, 3))):
                index, code = row(("pack", way, w)), row(("from", w))
                tile = _take(merged[sources[0]], index)
                for t in sources[1:]:
                    tile = jnp.where(code == t, _take(merged[t], index), tile)
                out_ref[md, h, w] = tile


def _sweep_kernel(
    jj_ref, c1_ref, c2_ref, table_ref, near_ref, own_ref, left_ref, right_ref,
    out_ref, sl_ref, u_ref, w_ref, f_ref, up_ref, a_ref, b_ref,
):
    lane = _lane()
    y = lax.broadcasted_iota(jnp.int32, (1, Y, 128), 1)
    inner_up = (y > 0).astype(F32)
    inner_down = (y < Y - 1).astype(F32)

    def row(name):
        return jnp.broadcast_to(table_ref[pl.ds(AT[name], 1), :], (Y, 128))

    def near(x):
        high = x.astype(jnp.bfloat16)
        rest = x - high.astype(F32)
        middle = rest.astype(jnp.bfloat16)
        low = (rest - middle.astype(F32)).astype(jnp.bfloat16)
        total = jnp.dot(
            jnp.concatenate([high, middle, low], axis=1), near_ref[...], preferred_element_type=F32
        )
        tiles = x.reshape(-1, Y, 128)
        along = pltpu.roll(tiles, 1, 1) * inner_up + pltpu.roll(tiles, Y - 1, 1) * inner_down
        return total + along.reshape(x.shape)

    from_left = (lane < 28) | ((lane >= 112) & (lane < 120))
    first = lane < 56
    second = (lane >= 56) & (lane < 84)

    def joined(left, right, a, b):
        tile = jnp.where(from_left, left, right)
        tile = jnp.where((lane >= 28) & first, a, tile)
        return jnp.where(second, b, tile)

    def f_parts(ref, md, h, j, index):
        tile = _take(ref[md, h, 2], index)
        if j >= 6:
            far = (lane < 14) | (lane >= 98)
            tile = jnp.where(far, _take(ref[md, h, j - 6], index), tile)
        return tile

    def unpack(md, _):
        for s in range(BLOCK + 1):
            t, r = divmod(s, 2)
            h, j = divmod(s, 8)
            a, b = own_ref[md, t], own_ref[PARTS + md, t]
            index = row(("g", j % 4))
            tile = joined(
                _take(left_ref[md, h, j // 4], index),
                _take(right_ref[md, h, j // 4], index),
                _roll(a, 28 - SLOT * r),
                _roll(b, 56 - SLOT * r),
            )
            if s == BLOCK:
                a_ref[pl.ds(md * Y, Y), :] = tile
                continue
            sl_ref[pl.ds((md * BLOCK + s) * 16, Y), :] = tile
            index = row(("f", j))
            f_ref[pl.ds((md * BLOCK + s) * Y, Y), :] = 2.0 * joined(
                f_parts(left_ref, md, h, j, index),
                f_parts(right_ref, md, h, j, index),
                _roll(a, -SLOT * r),
                _roll(b, 28 - SLOT * r),
            )
        return 0

    lax.fori_loop(0, PARTS, unpack, 0)
    b_ref[pl.ds(0, TERMS * Y), :] = 6.0 * a_ref[...] + near(a_ref[...])
    inside = a_ref[pl.ds(0, Y), :] > 0.0
    scale = jnp.where(inside, 1.0 / jnp.where(inside, b_ref[pl.ds(0, Y), :], 1.0), 0.0)

    chunk = 24

    def sweep(_, carry):
        for first_mode in range(0, MODES, chunk):
            x = jnp.concatenate([sl_ref[16 * j : 16 * j + Y] for j in range(first_mode, first_mode + chunk)])
            x = near(x)
            for n in range(chunk):
                sl_ref[16 * (first_mode + n) + Y : 16 * (first_mode + n) + 16] = x[Y * n : Y * n + Y]

        def mix(i, _):
            mine = sl_ref[pl.ds(i * 16, Y), :]
            a, b = a_ref[0:Y], b_ref[0:Y]
            u = a * mine
            v = b * mine - a * sl_ref[pl.ds(i * 16 + Y, Y), :]
            for k in range(1, TERMS):
                at = i * (TERMS - 1) + (k - 1)
                jj, c1, c2 = jj_ref[at], c1_ref[at], c2_ref[at]
                j1 = pl.multiple_of(jj & 0xFFFF, 16)
                j2 = pl.multiple_of(jj >> 16, 16)
                m = c1 * sl_ref[pl.ds(j1, Y), :] + c2 * sl_ref[pl.ds(j2, Y), :]
                lm = c1 * sl_ref[pl.ds(j1 + Y, Y), :] + c2 * sl_ref[pl.ds(j2 + Y, Y), :]
                a, b = a_ref[Y * k : Y * k + Y], b_ref[Y * k : Y * k + Y]
                u = u + a * m
                v = v + (b * m - a * lm)
            u_ref[pl.ds(i * Y, Y), :] = u
            w_ref[pl.ds(i * Y, Y), :] = f_ref[pl.ds(i * Y, Y), :] - v
            return 0

        lax.fori_loop(0, MODES, mix, 0, unroll=4)
        for first_mode in range(0, MODES, chunk):
            rows = pl.ds(first_mode * Y, chunk * Y)
            x = (w_ref[rows, :] + near(u_ref[rows, :])).reshape(chunk, Y, 128) * scale[None]
            for n in range(chunk):
                j = first_mode + n
                up_ref[Y * j : Y * j + Y] = x[n]
                sl_ref[16 * j : 16 * j + Y] = sl_ref[16 * j : 16 * j + Y] + 0.5 * x[n]
        return carry

    lax.fori_loop(0, ITERS, sweep, 0)
    home = (lane >= 28) & (lane < 84)

    def pack(md, _):
        both = []
        for m in range(BLOCK):
            i = md * BLOCK + m
            both.append(jnp.where(home, sl_ref[pl.ds(i * 16, Y), :], _roll(up_ref[pl.ds(i * Y, Y), :], 64)))
        for slab in range(SLABS):
            index = row(("own", slab))
            for t in range(4):
                tile = _take(both[4 * t], index)
                for r in range(1, 4):
                    if 4 * t + r < BLOCK:
                        tile = jnp.where(lane >= 32 * r, _take(both[4 * t + r], index), tile)
                out_ref[slab * PARTS + md, t] = tile
        return 0

    lax.fori_loop(0, PARTS, pack, 0)


def _receive_kernel(piece_ref, solution_ref, update_ref):
    lane = _lane()
    for t in range(4):
        rolled = [_roll(piece_ref[q, t], ZW * q) for q in range(GROUP)]
        for h in range(GROUP):
            m, n = 4 * t + h // 4, h % 4
            if m >= BLOCK:
                continue
            shifted = (lane - ZW * h) & 127
            tile = rolled[0]
            for q in range(1, GROUP):
                tile = jnp.where(shifted >= ZW * q, rolled[q], tile)
            (solution_ref, update_ref)[n // 2][m, n % 2] = _roll(tile, -ZW * h)


def _vmem(count):
    return [pl.BlockSpec(memory_space=pltpu.VMEM)] * count


def _smem(count):
    return [pl.BlockSpec(memory_space=pltpu.SMEM)] * count


def pattern_tables(triples, coupling):
    entries = coupling.shape[0]
    key = triples[0] * (TERMS - 1) + triples[2] - 1
    slots = lax.iota(jnp.int32, MODES * (TERMS - 1))
    code = lax.iota(jnp.int32, entries) * 128 + triples[1]
    match = key[:, None] == slots[None, :]
    low = jnp.min(jnp.where(match, code[:, None], entries * 128), axis=0)
    high = jnp.max(jnp.where(match, code[:, None], -1), axis=0)
    c1 = jnp.sum(jnp.where(code[:, None] == low[None, :], coupling[:, None], 0.0), axis=0)
    c2 = jnp.sum(jnp.where(code[:, None] == high[None, :], coupling[:, None], 0.0), axis=0)
    return (low & 127) * 16 + (high & 127) * (16 << 16), c1, c2


def per_device(guess, source, mean_coef, fluct_coef, triples, coupling):
    tile = (Y, 128)
    table = jnp.asarray(TABLE)
    which = lax.axis_index("mode").astype(jnp.int32).reshape(1)
    message = pl.pallas_call(
        _send_kernel,
        out_shape=jax.ShapeDtypeStruct((GROUP, PARTS) + tile, F32),
        in_specs=_smem(1) + _vmem(4),
        out_specs=_vmem(1)[0],
        name="send",
    )(which, guess, source, mean_coef, fluct_coef)
    block = lax.all_to_all(message, ("slab", "mode"), 0, 0, tiled=True)
    to_right, to_left = pl.pallas_call(
        _halo_kernel,
        out_shape=[jax.ShapeDtypeStruct((PARTS, 2, 3) + tile, F32)] * 2,
        in_specs=_vmem(2),
        out_specs=_vmem(2),
        name="halo",
    )(table, block)
    count = lax.axis_size("pair")
    from_left = lax.ppermute(to_right, "pair", [(n, n + 1) for n in range(count - 1)])
    from_right = lax.ppermute(to_left, "pair", [(n + 1, n) for n in range(count - 1)])
    jj, c1, c2 = pattern_tables(triples, coupling)
    result = pl.pallas_call(
        _sweep_kernel,
        out_shape=jax.ShapeDtypeStruct((GROUP, 4) + tile, F32),
        in_specs=_smem(3) + _vmem(5),
        out_specs=_vmem(1)[0],
        scratch_shapes=[pltpu.VMEM((MODES * 16, 128), F32)]
        + [pltpu.VMEM((MODES * Y, 128), F32)] * 4
        + [pltpu.VMEM((TERMS * Y, 128), F32)] * 2,
        name="sweeps",
    )(jj, c1, c2, table, jnp.asarray(NEAR, jnp.bfloat16), block, from_left, from_right)
    pieces = lax.all_to_all(result, ("slab", "mode"), 0, 0, tiled=True)
    return tuple(
        pl.pallas_call(
            _receive_kernel,
            out_shape=[jax.ShapeDtypeStruct(guess.shape, F32)] * 2,
            in_specs=_vmem(1),
            out_specs=_vmem(2),
            name="receive",
        )(pieces)
    )


def solution(mesh):
    slabs, parts = mesh.devices.shape
    grouped = Mesh(mesh.devices.reshape(slabs // SLABS, SLABS, parts), ("pair", "slab", "mode"))
    x = ("pair", "slab")
    in_specs = (P("mode", x), P("mode", x), P(x), P(None, x), P(), P())
    out_specs = (P("mode", x), P("mode", x))
    return jax.shard_map(
        per_device, mesh=grouped, in_specs=in_specs, out_specs=out_specs, check_vma=False
    )
```

```python
import functools

import jax
import jax.numpy as jnp
import numpy as np
from jax import lax
from jax.experimental import pallas as pl
from jax.experimental.pallas import tpu as pltpu
from jax.sharding import Mesh
from jax.sharding import PartitionSpec as P

ITERS = 3
SLABS = 2
PARTS = 8
GROUP = SLABS * PARTS
BLOCK = 15
MODES = 120
TERMS = 8
Y, Z = 8, 128
ZW = 8
PW = 14
SLOT = 64
F32 = jnp.float32


def _lane_of(plane, z):
    if plane == -3:
        return 112 + z
    if plane == 6:
        return 120 + z
    return PW * (plane + 2) + z + 3


def _near_matrix():
    cells = {}
    for plane in range(-2, 6):
        for z in range(-3, 11):
            cells[plane, z] = _lane_of(plane, z)
    for plane in (-3, 6):
        for z in range(ZW):
            cells[plane, z] = _lane_of(plane, z)
    near = np.zeros((128, 128), np.float32)
    for (plane, z), lane in cells.items():
        for cell in ((plane + 1, z), (plane - 1, z), (plane, z + 1), (plane, z - 1)):
            if cell in cells:
                near[cells[cell], lane] = 1.0
    return np.concatenate([near] * 3, axis=0)


G_PARTS = ((-2, 12), (-1, 10), (0, 8))
F_PARTS = ((-1, 10), (0, 8))
G_FROM = {"right": (PW + 1, 2, 56), "left": (1, PW + 2, 56)}
F_FROM = {"right": (3 * PW + 2, 2 * PW + 3), "left": (2 * PW + 2, 3 * PW + 3)}


def _tables():
    rows, at = [], {}

    def add(name, fill):
        row = np.zeros(128, np.int32)
        for lane, value in fill:
            row[lane] = value
        at[name] = len(rows)
        rows.append(row)

    def f_place(j):
        if j < 6:
            return (2, 18 * j), (2, 18 * j + 10)
        return (2, 108 + 10 * (j - 6)), (j - 6, 120)

    for way in ("right", "left"):
        index = [[], [], []]
        source = [[], [], []]
        for j in range(8):
            base, row = SLOT * (j % 2), j // 2
            lane = 30 * (j % 4)
            for start, (_, width) in zip(G_FROM[way], G_PARTS):
                for t in range(width):
                    index[j // 4].append((lane, base + start + t))
                    source[j // 4].append((lane, row))
                    lane += 1
            for start, (_, width), (tile, lane) in zip(F_FROM[way], F_PARTS, f_place(j)):
                for t in range(width):
                    index[tile].append((lane + t, base + start + t))
                    source[tile].append((lane + t, row))
        for w in range(3):
            add(("pack", way, w), index[w])
            add(("from", w), source[w])
    sides = ((-1, -2, -3), (4, 5, 6))
    for pos in range(4):
        fill = []
        for planes in sides:
            lane = 30 * pos
            for plane, (low, width) in zip(planes, G_PARTS):
                for t in range(width):
                    fill.append((_lane_of(plane, low + t), lane))
                    lane += 1
        add(("g", pos), fill)
    for j in range(8):
        fill = []
        for planes in sides:
            for plane, (low, width), (_, lane) in zip(planes, F_PARTS, f_place(j)):
                fill += [(_lane_of(plane, low + t), lane + t) for t in range(width)]
        add(("f", j), fill)
    for slab in range(SLABS):
        fill = []
        for lane in range(128):
            part, z = lane % 32 // ZW, lane % ZW
            home = _lane_of(SLABS * slab + part % 2, z)
            fill.append((lane, (home + SLOT * (part // 2)) % 128))
        add(("own", slab), fill)
    while len(rows) % 8:
        rows.append(np.zeros(128, np.int32))
    return np.stack(rows), at


TABLE, AT = _tables()
NEAR = _near_matrix()


def _take(tile, index):
    return jnp.take_along_axis(tile, index, axis=1, mode="promise_in_bounds")


def _lane():
    return lax.broadcasted_iota(jnp.int32, (Y, 128), 1)


def _roll(tile, amount):
    amount %= 128
    return pltpu.roll(tile, amount, 1) if amount else tile


def _send_kernel(which_ref, guess_ref, source_ref, mean_ref, fluct_ref, out_ref):
    lane = _lane()
    off = lane % SLOT % PW - 3
    which = which_ref[0]
    other = jnp.maximum(which - 1, 0)
    for t in range(PARTS):
        pieces = []
        for r in range(2):
            m = 2 * t + r
            if m < BLOCK:
                four = (guess_ref[m, 0], guess_ref[m, 1], source_ref[m, 0], source_ref[m, 1])
            else:
                four = tuple(jnp.where(which == 0, mean_ref[p], fluct_ref[other, p]) for p in range(2))
            for n, piece in enumerate(four):
                start = SLOT * r + PW * n
                pieces.append((start, _roll(piece, start + 3)))
        for q in range(GROUP):
            shifted = (lane - ZW * q) & 127
            tile = pieces[0][1]
            for start, piece in pieces[1:]:
                tile = jnp.where(shifted >= start, piece, tile)
            tile = _roll(tile, -ZW * q)
            if q == 0:
                tile = jnp.where(off < 0, 0.0, tile)
            if q == GROUP - 1:
                tile = jnp.where(off >= ZW, 0.0, tile)
            out_ref[q, t] = tile


def _halo_kernel(way, table_ref, block_ref, out_ref):
    spare = _lane() % SLOT >= 4 * PW
    home, away, shift = (PARTS, 0, 56 - 17) if way == "right" else (0, PARTS, 56 - 3)
    merged = [
        [
            jnp.where(spare, _roll(block_ref[away + md, t], shift), block_ref[home + md, t])
            for t in range(PARTS)
        ]
        for md in range(PARTS)
    ]
    for w, sources in ((0, (0, 1, 3)), (1, (2, 3)), (2, (0, 1, 2, 3))):
        index = jnp.broadcast_to(table_ref[pl.ds(AT["pack", way, w], 1), :], (Y, 128))
        code = jnp.broadcast_to(table_ref[pl.ds(AT["from", w], 1), :], (Y, 128))
        for md in range(PARTS):
            for h in range(2):
                tile = _take(merged[md][4 * h + sources[0]], index)
                for t in sources[1:]:
                    tile = jnp.where(code == t, _take(merged[md][4 * h + t], index), tile)
                out_ref[md, h, w] = tile


def _own_kernel(block_ref, s_ref, f_ref, a_ref):
    lane = _lane()
    first = lane < 56
    for md in range(PARTS):
        for s in range(BLOCK + 1):
            t, r = divmod(s, 2)
            a, b = block_ref[md, t], block_ref[PARTS + md, t]
            tile = jnp.where(first, _roll(a, 28 - SLOT * r), _roll(b, 56 - SLOT * r))
            if s == BLOCK:
                a_ref[md] = tile
                continue
            s_ref[md * BLOCK + s] = tile
            f_ref[md * BLOCK + s] = jnp.where(first, _roll(a, -SLOT * r), _roll(b, 28 - SLOT * r))


def _sweep_kernel(
    jj_ref, c1_ref, c2_ref, table_ref, near_ref, own_s_ref, own_f_ref, own_a_ref, left_ref, right_ref,
    out_ref, sl_ref, u_ref, w_ref, f_ref, up_ref, a_ref, b_ref,
):
    lane = _lane()
    y = lax.broadcasted_iota(jnp.int32, (1, Y, 128), 1)
    inner_up = (y > 0).astype(F32)
    inner_down = (y < Y - 1).astype(F32)

    def row(name):
        return jnp.broadcast_to(table_ref[pl.ds(AT[name], 1), :], (Y, 128))

    def near(x):
        high = x.astype(jnp.bfloat16)
        rest = x - high.astype(F32)
        middle = rest.astype(jnp.bfloat16)
        low = (rest - middle.astype(F32)).astype(jnp.bfloat16)
        total = jnp.dot(
            jnp.concatenate([high, middle, low], axis=1), near_ref[...], preferred_element_type=F32
        )
        tiles = x.reshape(-1, Y, 128)
        along = pltpu.roll(tiles, 1, 1) * inner_up + pltpu.roll(tiles, Y - 1, 1) * inner_down
        return total + along.reshape(x.shape)

    from_left = (lane < 28) | ((lane >= 112) & (lane < 120))
    own = (lane >= 28) & (lane < 84)
    far = (lane < 14) | (lane >= 98)

    for j in range(8):
        g_index, f_index = row(("g", j % 4)), row(("f", j))
        for md in range(PARTS):
            for h in range(2):
                m = md * BLOCK + 8 * h + j
                sides = [_take(ref[md, h, j // 4], g_index) for ref in (left_ref, right_ref)]
                tile = jnp.where(from_left, sides[0], sides[1])
                if 8 * h + j == BLOCK:
                    a_ref[Y * md : Y * md + Y] = jnp.where(own, own_a_ref[md], tile)
                else:
                    sl_ref[16 * m : 16 * m + Y] = jnp.where(own, own_s_ref[m], tile)
        for md in range(PARTS):
            for h in range(2):
                m = md * BLOCK + 8 * h + j
                if 8 * h + j == BLOCK:
                    continue
                sides = []
                for ref in (left_ref, right_ref):
                    side = _take(ref[md, h, 2], f_index)
                    if j >= 6:
                        side = jnp.where(far, _take(ref[md, h, j - 6], f_index), side)
                    sides.append(side)
                tile = jnp.where(from_left, sides[0], sides[1])
                f_ref[Y * m : Y * m + Y] = 2.0 * jnp.where(own, own_f_ref[m], tile)
    b_ref[pl.ds(0, TERMS * Y), :] = 6.0 * a_ref[...] + near(a_ref[...])
    inside = a_ref[pl.ds(0, Y), :] > 0.0
    scale = jnp.where(inside, 1.0 / jnp.where(inside, b_ref[pl.ds(0, Y), :], 1.0), 0.0)

    chunk = 24

    def sweep(_, carry):
        for first_mode in range(0, MODES, chunk):
            x = jnp.concatenate([sl_ref[16 * j : 16 * j + Y] for j in range(first_mode, first_mode + chunk)])
            x = near(x)
            for n in range(chunk):
                sl_ref[16 * (first_mode + n) + Y : 16 * (first_mode + n) + 16] = x[Y * n : Y * n + Y]

        def mix(i, _):
            mine = sl_ref[pl.ds(i * 16, Y), :]
            a, b = a_ref[0:Y], b_ref[0:Y]
            u = a * mine
            v = b * mine - a * sl_ref[pl.ds(i * 16 + Y, Y), :]
            for k in range(1, TERMS):
                at = i * (TERMS - 1) + (k - 1)
                jj, c1, c2 = jj_ref[at], c1_ref[at], c2_ref[at]
                j1 = pl.multiple_of(jj & 0xFFFF, 16)
                j2 = pl.multiple_of(jj >> 16, 16)
                m = c1 * sl_ref[pl.ds(j1, Y), :] + c2 * sl_ref[pl.ds(j2, Y), :]
                lm = c1 * sl_ref[pl.ds(j1 + Y, Y), :] + c2 * sl_ref[pl.ds(j2 + Y, Y), :]
                a, b = a_ref[Y * k : Y * k + Y], b_ref[Y * k : Y * k + Y]
                u = u + a * m
                v = v + (b * m - a * lm)
            u_ref[pl.ds(i * Y, Y), :] = u
            w_ref[pl.ds(i * Y, Y), :] = f_ref[pl.ds(i * Y, Y), :] - v
            return 0

        lax.fori_loop(0, MODES, mix, 0, unroll=8)
        for first_mode in range(0, MODES, chunk):
            rows = pl.ds(first_mode * Y, chunk * Y)
            x = (w_ref[rows, :] + near(u_ref[rows, :])).reshape(chunk, Y, 128) * scale[None]
            for n in range(chunk):
                j = first_mode + n
                up_ref[Y * j : Y * j + Y] = x[n]
                sl_ref[16 * j : 16 * j + Y] = sl_ref[16 * j : 16 * j + Y] + 0.5 * x[n]
        return carry

    lax.fori_loop(0, ITERS, sweep, 0)
    home = (lane >= 28) & (lane < 84)

    def pack(md, _):
        both = []
        for m in range(BLOCK):
            i = md * BLOCK + m
            both.append(jnp.where(home, sl_ref[pl.ds(i * 16, Y), :], _roll(up_ref[pl.ds(i * Y, Y), :], 64)))
        for slab in range(SLABS):
            index = row(("own", slab))
            for t in range(4):
                tile = _take(both[4 * t], index)
                for r in range(1, 4):
                    if 4 * t + r < BLOCK:
                        tile = jnp.where(lane >= 32 * r, _take(both[4 * t + r], index), tile)
                out_ref[slab * PARTS + md, t] = tile
        return 0

    lax.fori_loop(0, PARTS, pack, 0)


def _receive_kernel(piece_ref, solution_ref, update_ref):
    lane = _lane()
    for t in range(4):
        rolled = [_roll(piece_ref[q, t], ZW * q) for q in range(GROUP)]
        for h in range(GROUP):
            m, n = 4 * t + h // 4, h % 4
            if m >= BLOCK:
                continue
            shifted = (lane - ZW * h) & 127
            tile = rolled[0]
            for q in range(1, GROUP):
                tile = jnp.where(shifted >= ZW * q, rolled[q], tile)
            (solution_ref, update_ref)[n // 2][m, n % 2] = _roll(tile, -ZW * h)


def _vmem(count):
    return [pl.BlockSpec(memory_space=pltpu.VMEM)] * count


def _smem(count):
    return [pl.BlockSpec(memory_space=pltpu.SMEM)] * count


def pattern_tables(triples, coupling):
    entries = coupling.shape[0]
    key = triples[0] * (TERMS - 1) + triples[2] - 1
    slots = lax.iota(jnp.int32, MODES * (TERMS - 1))
    code = lax.iota(jnp.int32, entries) * 128 + triples[1]
    match = key[:, None] == slots[None, :]
    low = jnp.min(jnp.where(match, code[:, None], entries * 128), axis=0)
    high = jnp.max(jnp.where(match, code[:, None], -1), axis=0)
    c1 = jnp.sum(jnp.where(code[:, None] == low[None, :], coupling[:, None], 0.0), axis=0)
    c2 = jnp.sum(jnp.where(code[:, None] == high[None, :], coupling[:, None], 0.0), axis=0)
    return (low & 127) * 16 + (high & 127) * (16 << 16), c1, c2


def _call(kernel, outs, smem, name, scratch=()):
    def run(*args):
        args = [
            x if n < smem or isinstance(x, _Plain) else pltpu.with_memory_space_constraint(x, pltpu.VMEM)
            for n, x in enumerate(args)
        ]
        return pl.pallas_call(
            kernel,
            out_shape=outs,
            in_specs=_smem(smem) + _vmem(len(args) - smem),
            out_specs=_vmem(len(outs)),
            scratch_shapes=scratch,
            name=name,
        )(*[x.value if isinstance(x, _Plain) else x for x in args])

    return run


class _Plain:
    def __init__(self, value):
        self.value = value


def per_device(guess, source, mean_coef, fluct_coef, triples, coupling):
    tile = (Y, 128)
    table = _Plain(jnp.asarray(TABLE))
    near = _Plain(jnp.asarray(NEAR, jnp.bfloat16))
    which = lax.axis_index("mode").astype(jnp.int32).reshape(1)

    def kept(*shape):
        return pltpu.VMEM(shape + tile, F32)

    given = [_Plain(x) for x in (guess, source, mean_coef, fluct_coef)]
    (message,) = _call(_send_kernel, [kept(GROUP, PARTS)], 1, "send")(which, *given)
    block = lax.all_to_all(message, ("slab", "mode"), 0, 0, tiled=True)
    count = lax.axis_size("pair")
    halo = [kept(PARTS, 2, 3)]
    (to_right,) = _call(functools.partial(_halo_kernel, "right"), halo, 0, "halo_right")(table, block)
    from_left = lax.ppermute(to_right, "pair", [(n, n + 1) for n in range(count - 1)])
    (to_left,) = _call(functools.partial(_halo_kernel, "left"), halo, 0, "halo_left")(table, block)
    from_right = lax.ppermute(to_left, "pair", [(n + 1, n) for n in range(count - 1)])
    own = _call(_own_kernel, [kept(MODES), kept(MODES), kept(TERMS)], 0, "own")(block)
    jj, c1, c2 = pattern_tables(triples, coupling)
    scratch = (
        [pltpu.VMEM((MODES * 16, 128), F32)]
        + [pltpu.VMEM((MODES * Y, 128), F32)] * 4
        + [pltpu.VMEM((TERMS * Y, 128), F32)] * 2
    )
    (result,) = _call(_sweep_kernel, [kept(GROUP, 4)], 3, "sweeps", scratch)(
        jj, c1, c2, table, near, *own, from_left, from_right
    )
    pieces = lax.all_to_all(result, ("slab", "mode"), 0, 0, tiled=True)
    outs = [jax.ShapeDtypeStruct(guess.shape, F32)] * 2
    return tuple(_call(_receive_kernel, outs, 0, "receive")(pieces))


def solution(mesh):
    slabs, parts = mesh.devices.shape
    grouped = Mesh(mesh.devices.reshape(slabs // SLABS, SLABS, parts), ("pair", "slab", "mode"))
    x = ("pair", "slab")
    in_specs = (P("mode", x), P("mode", x), P(x), P(None, x), P(), P())
    out_specs = (P("mode", x), P("mode", x))
    return jax.shard_map(
        per_device, mesh=grouped, in_specs=in_specs, out_specs=out_specs, check_vma=False
    )
```

```python
import functools

import jax
import jax.numpy as jnp
import numpy as np
from jax import lax
from jax.experimental import pallas as pl
from jax.experimental.pallas import tpu as pltpu
from jax.sharding import Mesh
from jax.sharding import PartitionSpec as P

ITERS = 3
SLABS = 2
PARTS = 8
GROUP = SLABS * PARTS
BLOCK = 15
MODES = 120
TERMS = 8
Y, Z = 8, 128
STEP = 8
ZW = 8
PW = 14
SLOT = 64
F32 = jnp.float32


def _lane_of(plane, z):
    if plane == -3:
        return 112 + z
    if plane == 6:
        return 120 + z
    return PW * (plane + 2) + z + 3


def _near_matrix():
    cells = {}
    for plane in range(-2, 6):
        for z in range(-3, 11):
            cells[plane, z] = _lane_of(plane, z)
    for plane in (-3, 6):
        for z in range(ZW):
            cells[plane, z] = _lane_of(plane, z)
    near = np.zeros((128, 128), np.float32)
    for (plane, z), lane in cells.items():
        for cell in ((plane + 1, z), (plane - 1, z), (plane, z + 1), (plane, z - 1)):
            if cell in cells:
                near[cells[cell], lane] = 1.0
    return np.concatenate([near] * 3, axis=0)


G_PARTS = ((-2, 12), (-1, 10), (0, 8))
F_PARTS = ((-1, 10), (0, 8))
G_FROM = {"right": (PW + 1, 2, 56), "left": (1, PW + 2, 56)}
F_FROM = {"right": (3 * PW + 2, 2 * PW + 3), "left": (2 * PW + 2, 3 * PW + 3)}


def _tables():
    rows, at = [], {}

    def add(name, fill):
        row = np.zeros(128, np.int32)
        for lane, value in fill:
            row[lane] = value
        at[name] = len(rows)
        rows.append(row)

    def f_place(j):
        if j < 6:
            return (2, 18 * j), (2, 18 * j + 10)
        return (2, 108 + 10 * (j - 6)), (j - 6, 120)

    for way in ("right", "left"):
        index = [[], [], []]
        source = [[], [], []]
        for j in range(8):
            base, row = SLOT * (j % 2), j // 2
            lane = 30 * (j % 4)
            for start, (_, width) in zip(G_FROM[way], G_PARTS):
                for t in range(width):
                    index[j // 4].append((lane, base + start + t))
                    source[j // 4].append((lane, row))
                    lane += 1
            for start, (_, width), (tile, lane) in zip(F_FROM[way], F_PARTS, f_place(j)):
                for t in range(width):
                    index[tile].append((lane + t, base + start + t))
                    source[tile].append((lane + t, row))
        for w in range(3):
            add(("pack", way, w), index[w])
            add(("from", w), source[w])
    sides = ((-1, -2, -3), (4, 5, 6))
    for pos in range(4):
        fill = []
        for planes in sides:
            lane = 30 * pos
            for plane, (low, width) in zip(planes, G_PARTS):
                for t in range(width):
                    fill.append((_lane_of(plane, low + t), lane))
                    lane += 1
        add(("g", pos), fill)
    for j in range(8):
        fill = []
        for planes in sides:
            for plane, (low, width), (_, lane) in zip(planes, F_PARTS, f_place(j)):
                fill += [(_lane_of(plane, low + t), lane + t) for t in range(width)]
        add(("f", j), fill)
    for slab in range(SLABS):
        fill = []
        for lane in range(128):
            part, z = lane % 32 // ZW, lane % ZW
            home = _lane_of(SLABS * slab + part % 2, z)
            fill.append((lane, (home + SLOT * (part // 2)) % 128))
        add(("own", slab), fill)
    while len(rows) % 8:
        rows.append(np.zeros(128, np.int32))
    return np.stack(rows), at


TABLE, AT = _tables()
NEAR = _near_matrix()


def _take(tile, index):
    return jnp.take_along_axis(tile, index, axis=1, mode="promise_in_bounds")


def _lane():
    return lax.broadcasted_iota(jnp.int32, (Y, 128), 1)


def _roll(tile, amount):
    amount %= 128
    return pltpu.roll(tile, amount, 1) if amount else tile


def _send_kernel(which_ref, guess_ref, source_ref, mean_ref, fluct_ref, out_ref):
    lane = _lane()
    off = lane % SLOT % PW - 3
    which = which_ref[0]
    other = jnp.maximum(which - 1, 0)
    for t in range(PARTS):
        pieces = []
        for r in range(2):
            m = 2 * t + r
            if m < BLOCK:
                four = (guess_ref[m, 0], guess_ref[m, 1], source_ref[m, 0], source_ref[m, 1])
            else:
                four = tuple(jnp.where(which == 0, mean_ref[p], fluct_ref[other, p]) for p in range(2))
            for n, piece in enumerate(four):
                start = SLOT * r + PW * n
                pieces.append((start, _roll(piece, start + 3)))
        for q in range(GROUP):
            shifted = (lane - ZW * q) & 127
            tile = pieces[0][1]
            for start, piece in pieces[1:]:
                tile = jnp.where(shifted >= start, piece, tile)
            tile = _roll(tile, -ZW * q)
            if q == 0:
                tile = jnp.where(off < 0, 0.0, tile)
            if q == GROUP - 1:
                tile = jnp.where(off >= ZW, 0.0, tile)
            out_ref[q, t] = tile


def _halo_kernel(way, table_ref, block_ref, out_ref):
    spare = _lane() % SLOT >= 4 * PW
    home, away, shift = (PARTS, 0, 56 - 17) if way == "right" else (0, PARTS, 56 - 3)
    merged = [
        [
            jnp.where(spare, _roll(block_ref[away + md, t], shift), block_ref[home + md, t])
            for t in range(PARTS)
        ]
        for md in range(PARTS)
    ]
    for w, sources in ((0, (0, 1, 3)), (1, (2, 3)), (2, (0, 1, 2, 3))):
        index = jnp.broadcast_to(table_ref[pl.ds(AT["pack", way, w], 1), :], (Y, 128))
        code = jnp.broadcast_to(table_ref[pl.ds(AT["from", w], 1), :], (Y, 128))
        for md in range(PARTS):
            for h in range(2):
                tile = _take(merged[md][4 * h + sources[0]], index)
                for t in sources[1:]:
                    tile = jnp.where(code == t, _take(merged[md][4 * h + t], index), tile)
                out_ref[md, h, w] = tile


def _own_kernel(block_ref, s_ref, f_ref, a_ref):
    lane = _lane()
    first = lane < 56
    for md in range(PARTS):
        for s in range(BLOCK + 1):
            t, r = divmod(s, 2)
            a, b = block_ref[md, t], block_ref[PARTS + md, t]
            tile = jnp.where(first, _roll(a, 28 - SLOT * r), _roll(b, 56 - SLOT * r))
            if s == BLOCK:
                a_ref[md] = tile
                continue
            s_ref[md * BLOCK + s] = tile
            f_ref[md * BLOCK + s] = jnp.where(first, _roll(a, -SLOT * r), _roll(b, 28 - SLOT * r))


def _values_kernel(c1_ref, c2_ref, out_ref):
    def body(n, _):
        for r in range(8):
            at = 8 * n + r
            out_ref[pl.ds(2 * at, 1), :] = jnp.full((1, 128), c1_ref[at])
            out_ref[pl.ds(2 * at + 1, 1), :] = jnp.full((1, 128), c2_ref[at])
        return 0

    lax.fori_loop(0, MODES * (TERMS - 1) // 8, body, 0)


def _sweep_kernel(
    j1_ref, j2_ref, value_ref, table_ref, near_ref, own_s_ref, own_f_ref, own_a_ref, left_ref, right_ref,
    out_ref, sl_ref, u_ref, w_ref, f_ref, up_ref, a_ref, b_ref,
):
    lane = _lane()
    y = lax.broadcasted_iota(jnp.int32, (1, Y, 128), 1)
    inner_up = (y > 0).astype(F32)
    inner_down = (y < Y - 1).astype(F32)

    def row(name):
        return jnp.broadcast_to(table_ref[pl.ds(AT[name], 1), :], (Y, 128))

    def value(at):
        return jnp.broadcast_to(value_ref[pl.ds(at, 1), :], (Y, 128))

    def near(x):
        high = x.astype(jnp.bfloat16)
        rest = x - high.astype(F32)
        middle = rest.astype(jnp.bfloat16)
        low = (rest - middle.astype(F32)).astype(jnp.bfloat16)
        total = jnp.dot(
            jnp.concatenate([high, middle, low], axis=1), near_ref[...], preferred_element_type=F32
        )
        tiles = x.reshape(-1, Y, 128)
        along = pltpu.roll(tiles, 1, 1) * inner_up + pltpu.roll(tiles, Y - 1, 1) * inner_down
        return total + along.reshape(x.shape)

    from_left = (lane < 28) | ((lane >= 112) & (lane < 120))
    own = (lane >= 28) & (lane < 84)
    far = (lane < 14) | (lane >= 98)

    for j in range(8):
        g_index, f_index = row(("g", j % 4)), row(("f", j))
        for md in range(PARTS):
            for h in range(2):
                m = md * BLOCK + 8 * h + j
                sides = [_take(ref[md, h, j // 4], g_index) for ref in (left_ref, right_ref)]
                tile = jnp.where(from_left, sides[0], sides[1])
                if 8 * h + j == BLOCK:
                    a_ref[Y * md : Y * md + Y] = jnp.where(own, own_a_ref[md], tile)
                else:
                    sl_ref[16 * m : 16 * m + Y] = jnp.where(own, own_s_ref[m], tile)
        for md in range(PARTS):
            for h in range(2):
                m = md * BLOCK + 8 * h + j
                if 8 * h + j == BLOCK:
                    continue
                sides = []
                for ref in (left_ref, right_ref):
                    side = _take(ref[md, h, 2], f_index)
                    if j >= 6:
                        side = jnp.where(far, _take(ref[md, h, j - 6], f_index), side)
                    sides.append(side)
                tile = jnp.where(from_left, sides[0], sides[1])
                f_ref[Y * m : Y * m + Y] = 2.0 * jnp.where(own, own_f_ref[m], tile)
    b_ref[pl.ds(0, TERMS * Y), :] = 6.0 * a_ref[...] + near(a_ref[...])
    inside = a_ref[pl.ds(0, Y), :] > 0.0
    scale = jnp.where(inside, 1.0 / jnp.where(inside, b_ref[pl.ds(0, Y), :], 1.0), 0.0)

    chunk = 24

    def sweep(_, carry):
        for first_mode in range(0, MODES, chunk):
            x = jnp.concatenate([sl_ref[16 * j : 16 * j + Y] for j in range(first_mode, first_mode + chunk)])
            x = near(x)
            for n in range(chunk):
                sl_ref[16 * (first_mode + n) + Y : 16 * (first_mode + n) + 16] = x[Y * n : Y * n + Y]

        def mix(n, _):
            first_i = n * STEP
            modes = [first_i + r for r in range(STEP)]
            a, b = a_ref[0:Y], b_ref[0:Y]
            us, ws = [], []
            for i in modes:
                mine = sl_ref[pl.ds(i * 16, Y), :]
                us.append(a * mine)
                ws.append(f_ref[pl.ds(i * Y, Y), :] - (b * mine - a * sl_ref[pl.ds(i * 16 + Y, Y), :]))
            for k in range(1, TERMS):
                a, b = a_ref[Y * k : Y * k + Y], b_ref[Y * k : Y * k + Y]
                for r, i in enumerate(modes):
                    at = first_i * (TERMS - 1) + (r * (TERMS - 1) + k - 1)
                    j1, j2 = pl.multiple_of(j1_ref[at], 16), pl.multiple_of(j2_ref[at], 16)
                    c1, c2 = value(2 * at), value(2 * at + 1)
                    m = c1 * sl_ref[pl.ds(j1, Y), :] + c2 * sl_ref[pl.ds(j2, Y), :]
                    lm = c1 * sl_ref[pl.ds(j1 + Y, Y), :] + c2 * sl_ref[pl.ds(j2 + Y, Y), :]
                    us[r] = us[r] + a * m
                    ws[r] = ws[r] - (b * m - a * lm)
            for r, i in enumerate(modes):
                u_ref[pl.ds(i * Y, Y), :] = us[r]
                w_ref[pl.ds(i * Y, Y), :] = ws[r]
            return 0

        lax.fori_loop(0, MODES // STEP, mix, 0)
        for first_mode in range(0, MODES, chunk):
            rows = pl.ds(first_mode * Y, chunk * Y)
            x = (w_ref[rows, :] + near(u_ref[rows, :])).reshape(chunk, Y, 128) * scale[None]
            for n in range(chunk):
                j = first_mode + n
                up_ref[Y * j : Y * j + Y] = x[n]
                sl_ref[16 * j : 16 * j + Y] = sl_ref[16 * j : 16 * j + Y] + 0.5 * x[n]
        return carry

    lax.fori_loop(0, ITERS, sweep, 0)
    home = (lane >= 28) & (lane < 84)

    for slab in range(SLABS):
        index = row(("own", slab))
        for md in range(PARTS):
            for t in range(4):
                tile = None
                for r in range(4):
                    i = md * BLOCK + 4 * t + r
                    if 4 * t + r == BLOCK:
                        continue
                    if slab == 0:
                        both = jnp.where(home, sl_ref[16 * i : 16 * i + Y], _roll(up_ref[Y * i : Y * i + Y], 64))
                        u_ref[Y * i : Y * i + Y] = both
                    else:
                        both = u_ref[Y * i : Y * i + Y]
                    both = _take(both, index)
                    tile = both if r == 0 else jnp.where(lane >= 32 * r, both, tile)
                out_ref[slab * PARTS + md, t] = tile


def _receive_kernel(piece_ref, solution_ref, update_ref):
    lane = _lane()
    for t in range(4):
        rolled = [_roll(piece_ref[q, t], ZW * q) for q in range(GROUP)]
        for h in range(GROUP):
            m, n = 4 * t + h // 4, h % 4
            if m >= BLOCK:
                continue
            shifted = (lane - ZW * h) & 127
            tile = rolled[0]
            for q in range(1, GROUP):
                tile = jnp.where(shifted >= ZW * q, rolled[q], tile)
            (solution_ref, update_ref)[n // 2][m, n % 2] = _roll(tile, -ZW * h)


def _vmem(count):
    return [pl.BlockSpec(memory_space=pltpu.VMEM)] * count


def _smem(count):
    return [pl.BlockSpec(memory_space=pltpu.SMEM)] * count


def pattern_tables(triples, coupling):
    entries = coupling.shape[0]
    key = triples[0] * (TERMS - 1) + triples[2] - 1
    slots = lax.iota(jnp.int32, MODES * (TERMS - 1))
    code = lax.iota(jnp.int32, entries) * 128 + triples[1]
    match = key[:, None] == slots[None, :]
    low = jnp.min(jnp.where(match, code[:, None], entries * 128), axis=0)
    high = jnp.max(jnp.where(match, code[:, None], -1), axis=0)
    c1 = jnp.sum(jnp.where(code[:, None] == low[None, :], coupling[:, None], 0.0), axis=0)
    c2 = jnp.sum(jnp.where(code[:, None] == high[None, :], coupling[:, None], 0.0), axis=0)
    return (low & 127) * 16, (high & 127) * 16, c1, c2


def _call(kernel, outs, smem, name, scratch=()):
    def run(*args):
        args = [
            x if n < smem or isinstance(x, _Plain) else pltpu.with_memory_space_constraint(x, pltpu.VMEM)
            for n, x in enumerate(args)
        ]
        return pl.pallas_call(
            kernel,
            out_shape=outs,
            in_specs=_smem(smem) + _vmem(len(args) - smem),
            out_specs=_vmem(len(outs)),
            scratch_shapes=scratch,
            name=name,
        )(*[x.value if isinstance(x, _Plain) else x for x in args])

    return run


class _Plain:
    def __init__(self, value):
        self.value = value


def per_device(guess, source, mean_coef, fluct_coef, triples, coupling):
    tile = (Y, 128)
    table = _Plain(jnp.asarray(TABLE))
    near = _Plain(jnp.asarray(NEAR, jnp.bfloat16))
    which = lax.axis_index("mode").astype(jnp.int32).reshape(1)

    def kept(*shape):
        return pltpu.VMEM(shape + tile, F32)

    given = [_Plain(x) for x in (guess, source, mean_coef, fluct_coef)]
    (message,) = _call(_send_kernel, [kept(GROUP, PARTS)], 1, "send")(which, *given)
    block = lax.all_to_all(message, ("slab", "mode"), 0, 0, tiled=True)
    count = lax.axis_size("pair")
    halo = [kept(PARTS, 2, 3)]
    (to_right,) = _call(functools.partial(_halo_kernel, "right"), halo, 0, "halo_right")(table, block)
    from_left = lax.ppermute(to_right, "pair", [(n, n + 1) for n in range(count - 1)])
    (to_left,) = _call(functools.partial(_halo_kernel, "left"), halo, 0, "halo_left")(table, block)
    from_right = lax.ppermute(to_left, "pair", [(n + 1, n) for n in range(count - 1)])
    own = _call(_own_kernel, [kept(MODES), kept(MODES), kept(TERMS)], 0, "own")(block)
    triples, coupling, _ = lax.optimization_barrier((triples, coupling, to_right))
    j1, j2, c1, c2 = pattern_tables(triples, coupling)
    (values,) = _call(_values_kernel, [pltpu.VMEM((2 * MODES * (TERMS - 1), 128), F32)], 2, "values")(c1, c2)
    scratch = (
        [pltpu.VMEM((MODES * 16, 128), F32)]
        + [pltpu.VMEM((MODES * Y, 128), F32)] * 4
        + [pltpu.VMEM((TERMS * Y, 128), F32)] * 2
    )
    (result,) = _call(_sweep_kernel, [kept(GROUP, 4)], 2, "sweeps", scratch)(
        j1, j2, values, table, near, *own, from_left, from_right
    )
    pieces = lax.all_to_all(result, ("slab", "mode"), 0, 0, tiled=True)
    outs = [jax.ShapeDtypeStruct(guess.shape, F32)] * 2
    return tuple(_call(_receive_kernel, outs, 0, "receive")(pieces))


def solution(mesh):
    slabs, parts = mesh.devices.shape
    grouped = Mesh(mesh.devices.reshape(slabs // SLABS, SLABS, parts), ("pair", "slab", "mode"))
    x = ("pair", "slab")
    in_specs = (P("mode", x), P("mode", x), P(x), P(None, x), P(), P())
    out_specs = (P("mode", x), P("mode", x))
    return jax.shard_map(
        per_device, mesh=grouped, in_specs=in_specs, out_specs=out_specs, check_vma=False
    )
```

```python
import functools

import jax
import jax.numpy as jnp
import numpy as np
from jax import lax
from jax.experimental import pallas as pl
from jax.experimental.pallas import tpu as pltpu
from jax.sharding import Mesh
from jax.sharding import PartitionSpec as P

ITERS = 3
SLABS = 2
PARTS = 8
GROUP = SLABS * PARTS
BLOCK = 15
MODES = 120
TERMS = 8
Y, Z = 8, 128
STEP = 8
ZW = 8
PW = 14
SLOT = 64
F32 = jnp.float32


def _lane_of(plane, z):
    if plane == -3:
        return 112 + z
    if plane == 6:
        return 120 + z
    return PW * (plane + 2) + z + 3


def _near_matrix():
    cells = {}
    for plane in range(-2, 6):
        for z in range(-3, 11):
            cells[plane, z] = _lane_of(plane, z)
    for plane in (-3, 6):
        for z in range(ZW):
            cells[plane, z] = _lane_of(plane, z)
    near = np.zeros((128, 128), np.float32)
    for (plane, z), lane in cells.items():
        for cell in ((plane + 1, z), (plane - 1, z), (plane, z + 1), (plane, z - 1)):
            if cell in cells:
                near[cells[cell], lane] = 1.0
    return np.concatenate([near] * 3, axis=0)


G_PARTS = ((-2, 12), (-1, 10), (0, 8))
F_PARTS = ((-1, 10), (0, 8))
G_FROM = {"right": (PW + 1, 2, 56), "left": (1, PW + 2, 56)}
F_FROM = {"right": (3 * PW + 2, 2 * PW + 3), "left": (2 * PW + 2, 3 * PW + 3)}


def _tables():
    rows, at = [], {}

    def add(name, fill):
        row = np.zeros(128, np.int32)
        for lane, value in fill:
            row[lane] = value
        at[name] = len(rows)
        rows.append(row)

    def f_place(j):
        if j < 6:
            return (2, 18 * j), (2, 18 * j + 10)
        return (2, 108 + 10 * (j - 6)), (j - 6, 120)

    for way in ("right", "left"):
        index = [[], [], []]
        source = [[], [], []]
        for j in range(8):
            base, row = SLOT * (j % 2), j // 2
            lane = 30 * (j % 4)
            for start, (_, width) in zip(G_FROM[way], G_PARTS):
                for t in range(width):
                    index[j // 4].append((lane, base + start + t))
                    source[j // 4].append((lane, row))
                    lane += 1
            for start, (_, width), (tile, lane) in zip(F_FROM[way], F_PARTS, f_place(j)):
                for t in range(width):
                    index[tile].append((lane + t, base + start + t))
                    source[tile].append((lane + t, row))
        for w in range(3):
            add(("pack", way, w), index[w])
            add(("from", w), source[w])
    sides = ((-1, -2, -3), (4, 5, 6))
    for pos in range(4):
        fill = []
        for planes in sides:
            lane = 30 * pos
            for plane, (low, width) in zip(planes, G_PARTS):
                for t in range(width):
                    fill.append((_lane_of(plane, low + t), lane))
                    lane += 1
        add(("g", pos), fill)
    for j in range(8):
        fill = []
        for planes in sides:
            for plane, (low, width), (_, lane) in zip(planes, F_PARTS, f_place(j)):
                fill += [(_lane_of(plane, low + t), lane + t) for t in range(width)]
        add(("f", j), fill)
    for slab in range(SLABS):
        fill = []
        for lane in range(128):
            part, z = lane % 32 // ZW, lane % ZW
            home = _lane_of(SLABS * slab + part % 2, z)
            fill.append((lane, (home + SLOT * (part // 2)) % 128))
        add(("own", slab), fill)
    while len(rows) % 8:
        rows.append(np.zeros(128, np.int32))
    return np.stack(rows), at


TABLE, AT = _tables()
NEAR = _near_matrix()


def _take(tile, index):
    return jnp.take_along_axis(tile, index, axis=1, mode="promise_in_bounds")


def _lane():
    return lax.broadcasted_iota(jnp.int32, (Y, 128), 1)


def _roll(tile, amount):
    amount %= 128
    return pltpu.roll(tile, amount, 1) if amount else tile


def _send_kernel(which_ref, guess_ref, source_ref, mean_ref, fluct_ref, out_ref):
    lane = _lane()
    off = lane % SLOT % PW - 3
    which = which_ref[0]
    other = jnp.maximum(which - 1, 0)
    for t in range(PARTS):
        pieces = []
        for r in range(2):
            m = 2 * t + r
            if m < BLOCK:
                four = (guess_ref[m, 0], guess_ref[m, 1], source_ref[m, 0], source_ref[m, 1])
            else:
                four = tuple(jnp.where(which == 0, mean_ref[p], fluct_ref[other, p]) for p in range(2))
            for n, piece in enumerate(four):
                start = SLOT * r + PW * n
                pieces.append((start, _roll(piece, start + 3)))
        for q in range(GROUP):
            shifted = (lane - ZW * q) & 127
            tile = pieces[0][1]
            for start, piece in pieces[1:]:
                tile = jnp.where(shifted >= start, piece, tile)
            tile = _roll(tile, -ZW * q)
            if q == 0:
                tile = jnp.where(off < 0, 0.0, tile)
            if q == GROUP - 1:
                tile = jnp.where(off >= ZW, 0.0, tile)
            out_ref[q, t] = tile


def _halo_kernel(way, table_ref, block_ref, out_ref):
    spare = _lane() % SLOT >= 4 * PW
    home, away, shift = (PARTS, 0, 56 - 17) if way == "right" else (0, PARTS, 56 - 3)
    merged = [
        [
            jnp.where(spare, _roll(block_ref[away + md, t], shift), block_ref[home + md, t])
            for t in range(PARTS)
        ]
        for md in range(PARTS)
    ]
    for w, sources in ((0, (0, 1, 3)), (1, (2, 3)), (2, (0, 1, 2, 3))):
        index = jnp.broadcast_to(table_ref[pl.ds(AT["pack", way, w], 1), :], (Y, 128))
        code = jnp.broadcast_to(table_ref[pl.ds(AT["from", w], 1), :], (Y, 128))
        for md in range(PARTS):
            for h in range(2):
                tile = _take(merged[md][4 * h + sources[0]], index)
                for t in sources[1:]:
                    tile = jnp.where(code == t, _take(merged[md][4 * h + t], index), tile)
                out_ref[md, h, w] = tile


def _own_kernel(block_ref, s_ref, f_ref, a_ref):
    lane = _lane()
    first = lane < 56
    for md in range(PARTS):
        for s in range(BLOCK + 1):
            t, r = divmod(s, 2)
            a, b = block_ref[md, t], block_ref[PARTS + md, t]
            tile = jnp.where(first, _roll(a, 28 - SLOT * r), _roll(b, 56 - SLOT * r))
            if s == BLOCK:
                a_ref[md] = tile
                continue
            s_ref[md * BLOCK + s] = tile
            f_ref[md * BLOCK + s] = jnp.where(first, _roll(a, -SLOT * r), _roll(b, 28 - SLOT * r))


def _values_kernel(c1_ref, c2_ref, out_ref):
    def body(n, _):
        for r in range(8):
            at = 8 * n + r
            out_ref[pl.ds(2 * at, 1), :] = jnp.full((1, 128), c1_ref[at])
            out_ref[pl.ds(2 * at + 1, 1), :] = jnp.full((1, 128), c2_ref[at])
        return 0

    lax.fori_loop(0, MODES * (TERMS - 1) // 8, body, 0)


def _sweep_kernel(
    j1_ref, j2_ref, value_ref, table_ref, near_ref, own_s_ref, own_f_ref, own_a_ref, left_ref, right_ref,
    out_ref, sl_ref, u_ref, w_ref, f_ref, up_ref, a_ref, b_ref,
):
    lane = _lane()
    y = lax.broadcasted_iota(jnp.int32, (1, Y, 128), 1)
    inner_up = (y > 0).astype(F32)
    inner_down = (y < Y - 1).astype(F32)

    def row(name):
        return jnp.broadcast_to(table_ref[pl.ds(AT[name], 1), :], (Y, 128))

    def value(at):
        return jnp.broadcast_to(value_ref[pl.ds(at, 1), :], (Y, 128))

    def near(x):
        high = x.astype(jnp.bfloat16)
        rest = x - high.astype(F32)
        middle = rest.astype(jnp.bfloat16)
        low = (rest - middle.astype(F32)).astype(jnp.bfloat16)
        total = jnp.dot(
            jnp.concatenate([high, middle, low], axis=1), near_ref[...], preferred_element_type=F32
        )
        tiles = x.reshape(-1, Y, 128)
        along = pltpu.roll(tiles, 1, 1) * inner_up + pltpu.roll(tiles, Y - 1, 1) * inner_down
        return total + along.reshape(x.shape)

    from_left = (lane < 28) | ((lane >= 112) & (lane < 120))
    own = (lane >= 28) & (lane < 84)
    far = (lane < 14) | (lane >= 98)

    for j in range(8):
        g_index, f_index = row(("g", j % 4)), row(("f", j))
        for md in range(PARTS):
            for h in range(2):
                m = md * BLOCK + 8 * h + j
                sides = [_take(ref[md, h, j // 4], g_index) for ref in (left_ref, right_ref)]
                tile = jnp.where(from_left, sides[0], sides[1])
                if 8 * h + j == BLOCK:
                    a_ref[Y * md : Y * md + Y] = jnp.where(own, own_a_ref[md], tile)
                else:
                    sl_ref[16 * m : 16 * m + Y] = jnp.where(own, own_s_ref[m], tile)
        for md in range(PARTS):
            for h in range(2):
                m = md * BLOCK + 8 * h + j
                if 8 * h + j == BLOCK:
                    continue
                sides = []
                for ref in (left_ref, right_ref):
                    side = _take(ref[md, h, 2], f_index)
                    if j >= 6:
                        side = jnp.where(far, _take(ref[md, h, j - 6], f_index), side)
                    sides.append(side)
                tile = jnp.where(from_left, sides[0], sides[1])
                f_ref[Y * m : Y * m + Y] = 2.0 * jnp.where(own, own_f_ref[m], tile)
    b_ref[pl.ds(0, TERMS * Y), :] = 6.0 * a_ref[...] + near(a_ref[...])
    inside = a_ref[pl.ds(0, Y), :] > 0.0
    scale = jnp.where(inside, 1.0 / jnp.where(inside, b_ref[pl.ds(0, Y), :], 1.0), 0.0)

    chunk = 24

    def sweep(_, carry):
        for first_mode in range(0, MODES, chunk):
            x = jnp.concatenate([sl_ref[16 * j : 16 * j + Y] for j in range(first_mode, first_mode + chunk)])
            x = near(x)
            for n in range(chunk):
                sl_ref[16 * (first_mode + n) + Y : 16 * (first_mode + n) + 16] = x[Y * n : Y * n + Y]

        def mix(n, _):
            first_i = n * STEP
            modes = [first_i + r for r in range(STEP)]
            a, b = a_ref[0:Y], b_ref[0:Y]
            us, ws = [], []
            for i in modes:
                mine = sl_ref[pl.ds(i * 16, Y), :]
                us.append(a * mine)
                ws.append(f_ref[pl.ds(i * Y, Y), :] - (b * mine - a * sl_ref[pl.ds(i * 16 + Y, Y), :]))
            for k in range(1, TERMS):
                a, b = a_ref[Y * k : Y * k + Y], b_ref[Y * k : Y * k + Y]
                for r, i in enumerate(modes):
                    at = first_i * (TERMS - 1) + (r * (TERMS - 1) + k - 1)
                    j1, j2 = pl.multiple_of(j1_ref[at], 16), pl.multiple_of(j2_ref[at], 16)
                    c1, c2 = value(2 * at), value(2 * at + 1)
                    m = c1 * sl_ref[pl.ds(j1, Y), :] + c2 * sl_ref[pl.ds(j2, Y), :]
                    lm = c1 * sl_ref[pl.ds(j1 + Y, Y), :] + c2 * sl_ref[pl.ds(j2 + Y, Y), :]
                    us[r] = us[r] + a * m
                    ws[r] = ws[r] - (b * m - a * lm)
            for r, i in enumerate(modes):
                u_ref[pl.ds(i * Y, Y), :] = us[r]
                w_ref[pl.ds(i * Y, Y), :] = ws[r]
            return 0

        lax.fori_loop(0, MODES // STEP, mix, 0)
        for first_mode in range(0, MODES, chunk):
            rows = pl.ds(first_mode * Y, chunk * Y)
            x = (w_ref[rows, :] + near(u_ref[rows, :])).reshape(chunk, Y, 128) * scale[None]
            for n in range(chunk):
                j = first_mode + n
                up_ref[Y * j : Y * j + Y] = x[n]
                sl_ref[16 * j : 16 * j + Y] = sl_ref[16 * j : 16 * j + Y] + 0.5 * x[n]
        return carry

    lax.fori_loop(0, ITERS, sweep, 0)
    home = (lane >= 28) & (lane < 84)

    for slab in range(SLABS):
        index = row(("own", slab))
        for md in range(PARTS):
            for t in range(4):
                tile = None
                for r in range(4):
                    i = md * BLOCK + 4 * t + r
                    if 4 * t + r == BLOCK:
                        continue
                    if slab == 0:
                        both = jnp.where(home, sl_ref[16 * i : 16 * i + Y], _roll(up_ref[Y * i : Y * i + Y], 64))
                        u_ref[Y * i : Y * i + Y] = both
                    else:
                        both = u_ref[Y * i : Y * i + Y]
                    both = _take(both, index)
                    tile = both if r == 0 else jnp.where(lane >= 32 * r, both, tile)
                out_ref[slab * PARTS + md, t] = tile


def _receive_kernel(piece_ref, solution_ref, update_ref):
    lane = _lane()
    for t in range(4):
        rolled = [_roll(piece_ref[q, t], ZW * q) for q in range(GROUP)]
        for h in range(GROUP):
            m, n = 4 * t + h // 4, h % 4
            if m >= BLOCK:
                continue
            shifted = (lane - ZW * h) & 127
            tile = rolled[0]
            for q in range(1, GROUP):
                tile = jnp.where(shifted >= ZW * q, rolled[q], tile)
            (solution_ref, update_ref)[n // 2][m, n % 2] = _roll(tile, -ZW * h)


def _vmem(count):
    return [pl.BlockSpec(memory_space=pltpu.VMEM)] * count


def _smem(count):
    return [pl.BlockSpec(memory_space=pltpu.SMEM)] * count


def pattern_tables(triples, coupling):
    entries = coupling.shape[0]
    key = triples[0] * (TERMS - 1) + triples[2] - 1
    slots = lax.iota(jnp.int32, MODES * (TERMS - 1))
    code = lax.iota(jnp.int32, entries) * 128 + triples[1]
    match = key[:, None] == slots[None, :]
    low = jnp.min(jnp.where(match, code[:, None], entries * 128), axis=0)
    high = jnp.max(jnp.where(match, code[:, None], -1), axis=0)
    c1 = jnp.sum(jnp.where(code[:, None] == low[None, :], coupling[:, None], 0.0), axis=0)
    c2 = jnp.sum(jnp.where(code[:, None] == high[None, :], coupling[:, None], 0.0), axis=0)
    return (low & 127) * 16, (high & 127) * 16, c1, c2


def _call(kernel, outs, smem, name, scratch=()):
    def run(*args):
        args = [
            x if n < smem or isinstance(x, _Plain) else pltpu.with_memory_space_constraint(x, pltpu.VMEM)
            for n, x in enumerate(args)
        ]
        return pl.pallas_call(
            kernel,
            out_shape=outs,
            in_specs=_smem(smem) + _vmem(len(args) - smem),
            out_specs=_vmem(len(outs)),
            scratch_shapes=scratch,
            compiler_params=None if name == "send" else pltpu.CompilerParams(vmem_limit_bytes=24 << 20),
            name=name,
        )(*[x.value if isinstance(x, _Plain) else x for x in args])

    return run


class _Plain:
    def __init__(self, value):
        self.value = value


def per_device(guess, source, mean_coef, fluct_coef, triples, coupling):
    tile = (Y, 128)
    table = jnp.asarray(TABLE)
    near = _Plain(jnp.asarray(NEAR, jnp.bfloat16))
    which = lax.axis_index("mode").astype(jnp.int32).reshape(1)

    def kept(*shape):
        return pltpu.VMEM(shape + tile, F32)

    given = [_Plain(x) for x in (guess, source, mean_coef, fluct_coef)]
    (message,) = _call(_send_kernel, [kept(GROUP, PARTS)], 1, "send")(which, *given)
    block = lax.all_to_all(message, ("slab", "mode"), 0, 0, tiled=True)
    count = lax.axis_size("pair")
    halo = [kept(PARTS, 2, 3)]
    (to_right,) = _call(functools.partial(_halo_kernel, "right"), halo, 0, "halo_right")(table, block)
    from_left = lax.ppermute(to_right, "pair", [(n, n + 1) for n in range(count - 1)])
    (to_left,) = _call(functools.partial(_halo_kernel, "left"), halo, 0, "halo_left")(table, block)
    from_right = lax.ppermute(to_left, "pair", [(n + 1, n) for n in range(count - 1)])
    own = _call(_own_kernel, [kept(MODES), kept(MODES), kept(TERMS)], 0, "own")(block)
    triples, coupling, _ = lax.optimization_barrier((triples, coupling, to_right))
    j1, j2, c1, c2 = pattern_tables(triples, coupling)
    (values,) = _call(_values_kernel, [pltpu.VMEM((2 * MODES * (TERMS - 1), 128), F32)], 2, "values")(c1, c2)
    scratch = (
        [pltpu.VMEM((MODES * 16, 128), F32)]
        + [pltpu.VMEM((MODES * Y, 128), F32)] * 4
        + [pltpu.VMEM((TERMS * Y, 128), F32)] * 2
    )
    (result,) = _call(_sweep_kernel, [kept(GROUP, 4)], 2, "sweeps", scratch)(
        j1, j2, values, table, near, *own, from_left, from_right
    )
    pieces = lax.all_to_all(result, ("slab", "mode"), 0, 0, tiled=True)
    outs = [jax.ShapeDtypeStruct(guess.shape, F32)] * 2
    return tuple(_call(_receive_kernel, outs, 0, "receive")(pieces))


def solution(mesh):
    slabs, parts = mesh.devices.shape
    grouped = Mesh(mesh.devices.reshape(slabs // SLABS, SLABS, parts), ("pair", "slab", "mode"))
    x = ("pair", "slab")
    in_specs = (P("mode", x), P("mode", x), P(x), P(None, x), P(), P())
    out_specs = (P("mode", x), P("mode", x))
    return jax.shard_map(
        per_device, mesh=grouped, in_specs=in_specs, out_specs=out_specs, check_vma=False
    )
```

```python
import functools

import jax
import jax.numpy as jnp
import numpy as np
from jax import lax
from jax.experimental import pallas as pl
from jax.experimental.pallas import tpu as pltpu
from jax.sharding import Mesh
from jax.sharding import PartitionSpec as P

ITERS = 3
SLABS = 2
PARTS = 8
GROUP = SLABS * PARTS
BLOCK = 15
MODES = 120
TERMS = 8
Y, Z = 8, 128
STEP = 8
ZW = 8
PW = 14
SLOT = 64
F32 = jnp.float32


def _lane_of(plane, z):
    if plane == -3:
        return 112 + z
    if plane == 6:
        return 120 + z
    return PW * (plane + 2) + z + 3


def _near_matrix():
    cells = {}
    for plane in range(-2, 6):
        for z in range(-3, 11):
            cells[plane, z] = _lane_of(plane, z)
    for plane in (-3, 6):
        for z in range(ZW):
            cells[plane, z] = _lane_of(plane, z)
    near = np.zeros((128, 128), np.float32)
    for (plane, z), lane in cells.items():
        for cell in ((plane + 1, z), (plane - 1, z), (plane, z + 1), (plane, z - 1)):
            if cell in cells:
                near[cells[cell], lane] = 1.0
    return np.concatenate([near] * 3, axis=0)


G_PARTS = ((-2, 12), (-1, 10), (0, 8))
F_PARTS = ((-1, 10), (0, 8))
G_FROM = {"right": (PW + 1, 2, 56), "left": (1, PW + 2, 56)}
F_FROM = {"right": (3 * PW + 2, 2 * PW + 3), "left": (2 * PW + 2, 3 * PW + 3)}


def _tables():
    rows, at = [], {}

    def add(name, fill):
        row = np.zeros(128, np.int32)
        for lane, value in fill:
            row[lane] = value
        at[name] = len(rows)
        rows.append(row)

    def f_place(j):
        if j < 6:
            return (2, 18 * j), (2, 18 * j + 10)
        return (2, 108 + 10 * (j - 6)), (j - 6, 120)

    for way in ("right", "left"):
        index = [[], [], []]
        source = [[], [], []]
        for j in range(8):
            base, row = SLOT * (j % 2), j // 2
            lane = 30 * (j % 4)
            for start, (_, width) in zip(G_FROM[way], G_PARTS):
                for t in range(width):
                    index[j // 4].append((lane, base + start + t))
                    source[j // 4].append((lane, row))
                    lane += 1
            for start, (_, width), (tile, lane) in zip(F_FROM[way], F_PARTS, f_place(j)):
                for t in range(width):
                    index[tile].append((lane + t, base + start + t))
                    source[tile].append((lane + t, row))
        for w in range(3):
            add(("pack", way, w), index[w])
            add(("from", w), source[w])
    sides = ((-1, -2, -3), (4, 5, 6))
    for pos in range(4):
        fill = []
        for planes in sides:
            lane = 30 * pos
            for plane, (low, width) in zip(planes, G_PARTS):
                for t in range(width):
                    fill.append((_lane_of(plane, low + t), lane))
                    lane += 1
        add(("g", pos), fill)
    for j in range(8):
        fill = []
        for planes in sides:
            for plane, (low, width), (_, lane) in zip(planes, F_PARTS, f_place(j)):
                fill += [(_lane_of(plane, low + t), lane + t) for t in range(width)]
        add(("f", j), fill)
    for slab in range(SLABS):
        fill = []
        for lane in range(128):
            part, z = lane % 32 // ZW, lane % ZW
            home = _lane_of(SLABS * slab + part % 2, z)
            fill.append((lane, (home + SLOT * (part // 2)) % 128))
        add(("own", slab), fill)
    while len(rows) % 8:
        rows.append(np.zeros(128, np.int32))
    return np.stack(rows), at


TABLE, AT = _tables()
NEAR = _near_matrix()


def _take(tile, index):
    return jnp.take_along_axis(tile, index, axis=1, mode="promise_in_bounds")


def _lane():
    return lax.broadcasted_iota(jnp.int32, (Y, 128), 1)


def _roll(tile, amount):
    amount %= 128
    return pltpu.roll(tile, amount, 1) if amount else tile


def _send_kernel(which_ref, guess_ref, source_ref, mean_ref, fluct_ref, out_ref):
    lane = _lane()
    off = lane % SLOT % PW - 3
    which = which_ref[0]
    other = jnp.maximum(which - 1, 0)
    for t in range(PARTS):
        pieces = []
        for r in range(2):
            m = 2 * t + r
            if m < BLOCK:
                four = (guess_ref[m, 0], guess_ref[m, 1], source_ref[m, 0], source_ref[m, 1])
            else:
                four = tuple(jnp.where(which == 0, mean_ref[p], fluct_ref[other, p]) for p in range(2))
            for n, piece in enumerate(four):
                start = SLOT * r + PW * n
                pieces.append((start, _roll(piece, start + 3)))
        for q in range(GROUP):
            shifted = (lane - ZW * q) & 127
            tile = pieces[0][1]
            for start, piece in pieces[1:]:
                tile = jnp.where(shifted >= start, piece, tile)
            tile = _roll(tile, -ZW * q)
            if q == 0:
                tile = jnp.where(off < 0, 0.0, tile)
            if q == GROUP - 1:
                tile = jnp.where(off >= ZW, 0.0, tile)
            out_ref[q, t] = tile


def _halo_kernel(way, table_ref, block_ref, out_ref):
    spare = _lane() % SLOT >= 4 * PW
    home, away, shift = (PARTS, 0, 56 - 17) if way == "right" else (0, PARTS, 56 - 3)
    merged = [
        [
            jnp.where(spare, _roll(block_ref[away + md, t], shift), block_ref[home + md, t])
            for t in range(PARTS)
        ]
        for md in range(PARTS)
    ]
    for w, sources in ((0, (0, 1, 3)), (1, (2, 3)), (2, (0, 1, 2, 3))):
        index = jnp.broadcast_to(table_ref[pl.ds(AT["pack", way, w], 1), :], (Y, 128))
        code = jnp.broadcast_to(table_ref[pl.ds(AT["from", w], 1), :], (Y, 128))
        for md in range(PARTS):
            for h in range(2):
                tile = _take(merged[md][4 * h + sources[0]], index)
                for t in sources[1:]:
                    tile = jnp.where(code == t, _take(merged[md][4 * h + t], index), tile)
                out_ref[md, h, w] = tile


def _own_kernel(block_ref, s_ref, f_ref, a_ref):
    lane = _lane()
    first = lane < 56
    for md in range(PARTS):
        for s in range(BLOCK + 1):
            t, r = divmod(s, 2)
            a, b = block_ref[md, t], block_ref[PARTS + md, t]
            tile = jnp.where(first, _roll(a, 28 - SLOT * r), _roll(b, 56 - SLOT * r))
            if s == BLOCK:
                a_ref[md] = tile
                continue
            s_ref[md * BLOCK + s] = tile
            f_ref[md * BLOCK + s] = jnp.where(first, _roll(a, -SLOT * r), _roll(b, 28 - SLOT * r))


def _values_kernel(c1_ref, c2_ref, out_ref):
    def body(n, _):
        for r in range(8):
            at = 8 * n + r
            out_ref[pl.ds(2 * at, 1), :] = jnp.full((1, 128), c1_ref[at])
            out_ref[pl.ds(2 * at + 1, 1), :] = jnp.full((1, 128), c2_ref[at])
        return 0

    lax.fori_loop(0, MODES * (TERMS - 1) // 8, body, 0)


def _sweep_kernel(
    j1_ref, j2_ref, value_ref, table_ref, near_ref, own_s_ref, own_f_ref, own_a_ref, left_ref, right_ref,
    out_ref, sl_ref, u_ref, w_ref, f_ref, up_ref, a_ref, b_ref,
):
    lane = _lane()
    y = lax.broadcasted_iota(jnp.int32, (1, Y, 128), 1)
    inner_up = (y > 0).astype(F32)
    inner_down = (y < Y - 1).astype(F32)

    def row(name):
        return jnp.broadcast_to(table_ref[pl.ds(AT[name], 1), :], (Y, 128))

    def value(at):
        return jnp.broadcast_to(value_ref[pl.ds(at, 1), :], (Y, 128))

    def near(x):
        high = x.astype(jnp.bfloat16)
        rest = x - high.astype(F32)
        middle = rest.astype(jnp.bfloat16)
        low = (rest - middle.astype(F32)).astype(jnp.bfloat16)
        total = jnp.dot(
            jnp.concatenate([high, middle, low], axis=1), near_ref[...], preferred_element_type=F32
        )
        tiles = x.reshape(-1, Y, 128)
        along = pltpu.roll(tiles, 1, 1) * inner_up + pltpu.roll(tiles, Y - 1, 1) * inner_down
        return total + along.reshape(x.shape)

    from_left = (lane < 28) | ((lane >= 112) & (lane < 120))
    own = (lane >= 28) & (lane < 84)
    far = (lane < 14) | (lane >= 98)

    for j in range(8):
        g_index, f_index = row(("g", j % 4)), row(("f", j))
        for md in range(PARTS):
            for h in range(2):
                m = md * BLOCK + 8 * h + j
                sides = [_take(ref[md, h, j // 4], g_index) for ref in (left_ref, right_ref)]
                tile = jnp.where(from_left, sides[0], sides[1])
                if 8 * h + j == BLOCK:
                    a_ref[Y * md : Y * md + Y] = jnp.where(own, own_a_ref[md], tile)
                else:
                    sl_ref[16 * m : 16 * m + Y] = jnp.where(own, own_s_ref[m], tile)
        for md in range(PARTS):
            for h in range(2):
                m = md * BLOCK + 8 * h + j
                if 8 * h + j == BLOCK:
                    continue
                sides = []
                for ref in (left_ref, right_ref):
                    side = _take(ref[md, h, 2], f_index)
                    if j >= 6:
                        side = jnp.where(far, _take(ref[md, h, j - 6], f_index), side)
                    sides.append(side)
                tile = jnp.where(from_left, sides[0], sides[1])
                f_ref[Y * m : Y * m + Y] = 2.0 * jnp.where(own, own_f_ref[m], tile)
    b_ref[pl.ds(0, TERMS * Y), :] = 6.0 * a_ref[...] + near(a_ref[...])
    inside = a_ref[pl.ds(0, Y), :] > 0.0
    scale = jnp.where(inside, 1.0 / jnp.where(inside, b_ref[pl.ds(0, Y), :], 1.0), 0.0)

    chunk = 24

    def sweep(_, carry):
        for first_mode in range(0, MODES, chunk):
            x = jnp.concatenate([sl_ref[16 * j : 16 * j + Y] for j in range(first_mode, first_mode + chunk)])
            x = near(x)
            for n in range(chunk):
                sl_ref[16 * (first_mode + n) + Y : 16 * (first_mode + n) + 16] = x[Y * n : Y * n + Y]

        def mix(n, _):
            first_i = n * STEP
            modes = [first_i + r for r in range(STEP)]
            a, b = a_ref[0:Y], b_ref[0:Y]
            us, ws = [], []
            for i in modes:
                mine = sl_ref[pl.ds(i * 16, Y), :]
                us.append(a * mine)
                ws.append(f_ref[pl.ds(i * Y, Y), :] - (b * mine - a * sl_ref[pl.ds(i * 16 + Y, Y), :]))
            for k in range(1, TERMS):
                a, b = a_ref[Y * k : Y * k + Y], b_ref[Y * k : Y * k + Y]
                for r, i in enumerate(modes):
                    at = first_i * (TERMS - 1) + (r * (TERMS - 1) + k - 1)
                    j1, j2 = pl.multiple_of(j1_ref[at], 16), pl.multiple_of(j2_ref[at], 16)
                    c1, c2 = value(2 * at), value(2 * at + 1)
                    m = c1 * sl_ref[pl.ds(j1, Y), :] + c2 * sl_ref[pl.ds(j2, Y), :]
                    lm = c1 * sl_ref[pl.ds(j1 + Y, Y), :] + c2 * sl_ref[pl.ds(j2 + Y, Y), :]
                    us[r] = us[r] + a * m
                    ws[r] = ws[r] - (b * m - a * lm)
            for r, i in enumerate(modes):
                u_ref[pl.ds(i * Y, Y), :] = us[r]
                w_ref[pl.ds(i * Y, Y), :] = ws[r]
            return 0

        lax.fori_loop(0, MODES // STEP, mix, 0)
        for first_mode in range(0, MODES, chunk):
            rows = pl.ds(first_mode * Y, chunk * Y)
            x = (w_ref[rows, :] + near(u_ref[rows, :])).reshape(chunk, Y, 128) * scale[None]
            for n in range(chunk):
                j = first_mode + n
                up_ref[Y * j : Y * j + Y] = x[n]
                sl_ref[16 * j : 16 * j + Y] = sl_ref[16 * j : 16 * j + Y] + 0.5 * x[n]
        return carry

    lax.fori_loop(0, ITERS, sweep, 0)
    home = (lane >= 28) & (lane < 84)

    for slab in range(SLABS):
        index = row(("own", slab))
        for md in range(PARTS):
            for t in range(4):
                tile = None
                for r in range(4):
                    i = md * BLOCK + 4 * t + r
                    if 4 * t + r == BLOCK:
                        continue
                    if slab == 0:
                        both = jnp.where(home, sl_ref[16 * i : 16 * i + Y], _roll(up_ref[Y * i : Y * i + Y], 64))
                        u_ref[Y * i : Y * i + Y] = both
                    else:
                        both = u_ref[Y * i : Y * i + Y]
                    both = _take(both, index)
                    tile = both if r == 0 else jnp.where(lane >= 32 * r, both, tile)
                out_ref[slab * PARTS + md, t] = tile


def _receive_kernel(piece_ref, solution_ref, update_ref, kept_ref, sems):
    lane = _lane()
    copies = []
    for t in range(4):
        rolled = [_roll(piece_ref[q, t], ZW * q) for q in range(GROUP)]
        for h in range(GROUP):
            m, n = 4 * t + h // 4, h % 4
            if m >= BLOCK:
                continue
            shifted = (lane - ZW * h) & 127
            tile = rolled[0]
            for q in range(1, GROUP):
                tile = jnp.where(shifted >= ZW * q, rolled[q], tile)
            kept_ref[n // 2, m, n % 2] = _roll(tile, -ZW * h)
        part = pl.ds(4 * t, min(4, BLOCK - 4 * t))
        for n, out_ref in enumerate((solution_ref, update_ref)):
            copies.append(pltpu.make_async_copy(kept_ref.at[n, part], out_ref.at[part], sems.at[2 * t + n]))
            copies[-1].start()
    for copy in copies:
        copy.wait()


def _vmem(count):
    return [pl.BlockSpec(memory_space=pltpu.VMEM)] * count


def _smem(count):
    return [pl.BlockSpec(memory_space=pltpu.SMEM)] * count


def pattern_tables(triples, coupling):
    entries = coupling.shape[0]
    key = triples[0] * (TERMS - 1) + triples[2] - 1
    slots = lax.iota(jnp.int32, MODES * (TERMS - 1))
    code = lax.iota(jnp.int32, entries) * 128 + triples[1]
    match = key[:, None] == slots[None, :]
    low = jnp.min(jnp.where(match, code[:, None], entries * 128), axis=0)
    high = jnp.max(jnp.where(match, code[:, None], -1), axis=0)
    c1 = jnp.sum(jnp.where(code[:, None] == low[None, :], coupling[:, None], 0.0), axis=0)
    c2 = jnp.sum(jnp.where(code[:, None] == high[None, :], coupling[:, None], 0.0), axis=0)
    return (low & 127) * 16, (high & 127) * 16, c1, c2


def _call(kernel, outs, smem, name, scratch=()):
    def run(*args):
        args = [
            x if n < smem or isinstance(x, _Plain) else pltpu.with_memory_space_constraint(x, pltpu.VMEM)
            for n, x in enumerate(args)
        ]
        return pl.pallas_call(
            kernel,
            out_shape=outs,
            in_specs=_smem(smem) + _vmem(len(args) - smem),
            out_specs=_vmem(len(outs)),
            scratch_shapes=scratch,
            compiler_params=None if name == "send" else pltpu.CompilerParams(vmem_limit_bytes=24 << 20),
            name=name,
        )(*[x.value if isinstance(x, _Plain) else x for x in args])

    return run


class _Plain:
    def __init__(self, value):
        self.value = value


def per_device(guess, source, mean_coef, fluct_coef, triples, coupling):
    tile = (Y, 128)
    table = jnp.asarray(TABLE)
    near = _Plain(jnp.asarray(NEAR, jnp.bfloat16))
    which = lax.axis_index("mode").astype(jnp.int32).reshape(1)

    def kept(*shape):
        return pltpu.VMEM(shape + tile, F32)

    given = [_Plain(x) for x in (guess, source, mean_coef, fluct_coef)]
    (message,) = _call(_send_kernel, [kept(GROUP, PARTS)], 1, "send")(which, *given)
    block = lax.all_to_all(message, ("slab", "mode"), 0, 0, tiled=True)
    count = lax.axis_size("pair")
    halo = [kept(PARTS, 2, 3)]
    (to_right,) = _call(functools.partial(_halo_kernel, "right"), halo, 0, "halo_right")(table, block)
    from_left = lax.ppermute(to_right, "pair", [(n, n + 1) for n in range(count - 1)])
    (to_left,) = _call(functools.partial(_halo_kernel, "left"), halo, 0, "halo_left")(table, block)
    from_right = lax.ppermute(to_left, "pair", [(n + 1, n) for n in range(count - 1)])
    own = _call(_own_kernel, [kept(MODES), kept(MODES), kept(TERMS)], 0, "own")(block)
    triples, coupling, _ = lax.optimization_barrier((triples, coupling, to_right))
    j1, j2, c1, c2 = pattern_tables(triples, coupling)
    (values,) = _call(_values_kernel, [pltpu.VMEM((2 * MODES * (TERMS - 1), 128), F32)], 2, "values")(c1, c2)
    scratch = (
        [pltpu.VMEM((MODES * 16, 128), F32)]
        + [pltpu.VMEM((MODES * Y, 128), F32)] * 4
        + [pltpu.VMEM((TERMS * Y, 128), F32)] * 2
    )
    (result,) = _call(_sweep_kernel, [kept(GROUP, 4)], 2, "sweeps", scratch)(
        j1, j2, values, table, near, *own, from_left, from_right
    )
    pieces = lax.all_to_all(result, ("slab", "mode"), 0, 0, tiled=True)
    return tuple(
        pl.pallas_call(
            _receive_kernel,
            out_shape=[jax.ShapeDtypeStruct(guess.shape, F32)] * 2,
            in_specs=_vmem(1),
            out_specs=[pl.BlockSpec(memory_space=pl.ANY)] * 2,
            scratch_shapes=[pltpu.VMEM((2,) + guess.shape, F32), pltpu.SemaphoreType.DMA((8,))],
            compiler_params=pltpu.CompilerParams(vmem_limit_bytes=24 << 20),
            name="receive",
        )(pltpu.with_memory_space_constraint(pieces, pltpu.VMEM))
    )


def solution(mesh):
    slabs, parts = mesh.devices.shape
    grouped = Mesh(mesh.devices.reshape(slabs // SLABS, SLABS, parts), ("pair", "slab", "mode"))
    x = ("pair", "slab")
    in_specs = (P("mode", x), P("mode", x), P(x), P(None, x), P(), P())
    out_specs = (P("mode", x), P("mode", x))
    return jax.shard_map(
        per_device, mesh=grouped, in_specs=in_specs, out_specs=out_specs, check_vma=False
    )
```
